256 devices in a mesh: depth: 64 (over z, y, core), tile: 4 (over x).
Axes of the slice: x: 4, y: 4, z: 8, core: 2. Of those that a mesh axis runs over, the one named last changes fastest.
Arguments:
- density: float32 [128, 512, 2048], P('depth', 'tile'), may hold values from -6 to 6
- bins: int32 [128, 512, 2048], P('depth', 'tile'), may hold values from 0 to 255
- colors: bfloat16 [3, 256], replicated, may hold values from 0.099609375 to 1
- extinction: bfloat16 [256], replicated, may hold values from 0.049804688 to 20
Outputs:
- image: float32 [4, 512, 2048], P(None, 'tile', 'depth')
The draws below stay inside these ranges and needn't reach their ends.
All inputs are finite; a program needn't handle non-finite values.
Results may differ from the reference program's by a relative error of at most 0.0003.
Values sent between devices are 32-bit elements; how exact they have to be, the bound alone decides.
A program may use at most 256 MiB of HBM per device.

```python
import math
import jax
import jax.numpy as jnp
import numpy as np
from jax import lax

NZ = 2048
BINS = 256
NX = 128
NY = 512
SLABS = 64


def with_ends(values, rng, low, largest):
    longest = values.shape.index(max(values.shape))
    spots = []
    for shift in (0, 1):
        where = [jax.random.randint(jax.random.fold_in(rng, axis), (), 0, length) for axis, length in enumerate(values.shape)]
        where[longest] = (where[longest] + shift) % values.shape[longest]
        spots.append(tuple(where))
    return values.at[spots[0]].set(low).at[spots[1]].set(largest)


def shard_levels(key, extent, shards, smallest, high):
    def one(dim, shards_of):
        heights = jax.random.uniform(jax.random.fold_in(jax.random.fold_in(key, 6), dim), (shards_of,), jnp.float32, smallest / len(shards), high / len(shards))
        return jnp.repeat(jnp.exp(heights), extent[dim] // shards_of).reshape((-1,) + (1,) * (len(extent) - dim - 1))

    level = one(*shards[0])
    for cut in shards[1:]:
        level = level * one(*cut)
    return level


def bell_draw(stream_key, dims, spread, most, pieces=(), held_as=jnp.bfloat16):
    values = jax.random.normal(stream_key, dims, jnp.float32) * spread
    if len(pieces) > 0:
        values = shard_levels(stream_key, dims, pieces, -0.22, 0.18) * values
    return jnp.clip(values, min=-most, max=most).astype(held_as)


def setup_inputs(seed: int = 0) -> dict:
    seeds = jax.random.split(jax.random.key(seed), 5)
    density = bell_draw(seeds[0], (NX, NY, NZ), 1.0, 6.0, ((0, 64), (1, 4)), jnp.float32)
    bins = with_ends(jax.random.randint(seeds[1], (NX, NY, NZ), 0, BINS), jax.random.fold_in(seeds[1], 1), 0, BINS - 1).astype(jnp.int32)
    colors = jnp.clip(jax.random.uniform(seeds[2], (3, BINS), jnp.float32, 0.099609375, 1.0), 0.099609375, 1.0).astype(jnp.bfloat16)
    extinction = jnp.clip(jnp.exp(jax.random.uniform(seeds[3], (BINS,), jnp.float32, math.log(0.049804688), math.log(20.0))), 0.049804688, 20.0).astype(jnp.bfloat16)
    return dict(density=density, bins=bins, colors=colors, extinction=extinction)


def reversed_order(count):
    width_bits = count.bit_length() - 1
    result = []
    for index_j in range(count):
        value = 0
        for shift_k in range(width_bits):
            value = value | (index_j >> shift_k & 1) << width_bits - 1 - shift_k
        result.append(value)
    return np.array(result, dtype=np.int32)

def reference(density, bins, colors, extinction):
    lookup = jnp.concatenate([colors.astype(jnp.float32), extinction.astype(jnp.float32)[None, :]], 0)
    depth_scale = 0.6 / NX
    padded = jnp.pad(density, ((1, 1), (0, 0), (0, 0)))

    def plane_step(carry, index_x):
        radiance, running = carry
        before = lax.dynamic_slice_in_dim(padded, index_x, 1, 0)[0]
        center = lax.dynamic_slice_in_dim(padded, index_x + 1, 1, 0)[0]
        after = lax.dynamic_slice_in_dim(padded, index_x + 2, 1, 0)[0]
        grad_x = (after - before) * 0.5
        row_pad = jnp.pad(center, ((1, 1), (0, 0)))
        grad_y = (row_pad[2:] - row_pad[:-2]) * 0.5
        col_pad = jnp.pad(center, ((0, 0), (1, 1)))
        grad_z = (col_pad[:, 2:] - col_pad[:, :-2]) * 0.5
        lit = jnp.abs(0.48 * grad_x + 0.6 * grad_y + 0.64 * grad_z)
        shade = 0.3 + 0.7 * lit / jnp.sqrt(grad_x * grad_x + grad_y * grad_y + grad_z * grad_z + 1.0)
        plane_bins = lax.dynamic_slice_in_dim(bins, index_x, 1, 0)[0]
        entries = jnp.take(lookup, plane_bins, axis=1)
        optical = entries[3] * depth_scale
        emitted = entries[:3] * shade * (1.0 - jnp.exp(-optical))
        radiance = radiance + jnp.exp(-running) * emitted
        running = running + optical
        return ((radiance, running), None)
    start = (jnp.zeros((3, NY, NZ), jnp.float32), jnp.zeros((NY, NZ), jnp.float32))
    (radiance, running), unused = lax.scan(plane_step, start, jnp.arange(NX, dtype=jnp.int32))
    full = jnp.concatenate([radiance, (1.0 - jnp.exp(-running))[None]], 0)
    blocks = full.reshape(4, NY, SLABS, NZ // SLABS)
    blocks = blocks[:, :, reversed_order(SLABS), :]
    return blocks.reshape(4, NY, NZ)
```

```python
import functools

import jax
import jax.numpy as jnp
from jax import lax
from jax.experimental import pallas as pl
from jax.experimental.pallas import tpu as pltpu
from jax.sharding import PartitionSpec as P

ROW_BLOCK = 32
LANES = 128


def shift_pair(axis, count):
    return [(i, i + 1) for i in range(count - 1)], [(i + 1, i) for i in range(count - 1)]


def partner(value, axis, stride):
    return lax.ppermute(value, axis, [(i, i ^ 1 << stride) for i in range(lax.axis_size(axis))])


def over_pair(front, back):
    return jnp.concatenate([front[:3] + front[3:] * back[:3], front[3:] * back[3:]], 0)


def render_kernel(depth_scale, table_ref, d_ref, dprev_ref, dnext_ref, htop_ref, hbot_ref,
                  xp_ref, xn_ref, b_ref, out_ref):
    block = pl.program_id(0)
    last_block = pl.num_programs(0) - 1
    chunks = d_ref.shape[1] // 8
    groups = d_ref.shape[2] // LANES
    sub = lax.broadcasted_iota(jnp.int32, (8, LANES), 0)
    lane = lax.broadcasted_iota(jnp.int32, (8, LANES), 1)
    tables = [
        (jnp.broadcast_to(table_ref[ch:ch + 1, 0:LANES], (8, LANES)),
         jnp.broadcast_to(table_ref[ch:ch + 1, LANES:2 * LANES], (8, LANES)))
        for ch in range(4)
    ]

    def look(idx):
        low = idx & (LANES - 1)
        high = idx >= LANES
        vals = []
        for lo_t, hi_t in tables:
            lo_v = jnp.take_along_axis(lo_t, low, axis=1, mode="promise_in_bounds")
            hi_v = jnp.take_along_axis(hi_t, low, axis=1, mode="promise_in_bounds")
            vals.append(jnp.where(high, hi_v, lo_v))
        return vals

    def group_body(g, carry):
        col = pl.ds(pl.multiple_of(g * LANES, LANES), LANES)
        col_l = pl.ds(pl.multiple_of(jnp.maximum(g - 1, 0) * LANES, LANES), LANES)
        col_r = pl.ds(pl.multiple_of(jnp.minimum(g + 1, groups - 1) * LANES, LANES), LANES)
        has_l = g > 0
        has_r = g < groups - 1
        centers = [[d_ref[p, pl.ds(k * 8, 8), col] for k in range(chunks)] for p in range(2)]
        for k in range(chunks):
            rows = pl.ds(k * 8, 8)
            samples = []
            for p in range(2):
                c = centers[p][k]
                if k == 0:
                    up_src = jnp.where(block == 0, htop_ref[p, :, col], dprev_ref[p, :, col])
                else:
                    up_src = centers[p][k - 1]
                if k == chunks - 1:
                    dn_src = jnp.where(block == last_block, hbot_ref[p, :, col], dnext_ref[p, :, col])
                else:
                    dn_src = centers[p][k + 1]
                up = jnp.where(sub == 0, pltpu.roll(up_src, 1, 0), pltpu.roll(c, 1, 0))
                dn = jnp.where(sub == 7, pltpu.roll(dn_src, 7, 0), pltpu.roll(c, 7, 0))
                grad_y = (dn - up) * 0.5
                left_src = jnp.where(has_l, d_ref[p, rows, col_l], 0.0)
                right_src = jnp.where(has_r, d_ref[p, rows, col_r], 0.0)
                lf = jnp.where(lane == 0, pltpu.roll(left_src, 1, 1), pltpu.roll(c, 1, 1))
                rt = jnp.where(lane == LANES - 1, pltpu.roll(right_src, LANES - 1, 1),
                               pltpu.roll(c, LANES - 1, 1))
                grad_z = (rt - lf) * 0.5
                if p == 0:
                    grad_x = (centers[1][k] - xp_ref[rows, col]) * 0.5
                else:
                    grad_x = (xn_ref[rows, col] - centers[0][k]) * 0.5
                lit = jnp.abs(0.48 * grad_x + 0.6 * grad_y + 0.64 * grad_z)
                shade = 0.3 + 0.7 * lit / jnp.sqrt(
                    grad_x * grad_x + grad_y * grad_y + grad_z * grad_z + 1.0)
                entries = look(b_ref[p, rows, col])
                optical = entries[3] * depth_scale
                absorb = 1.0 - jnp.exp(-optical)
                emitted = [entries[ch] * shade * absorb for ch in range(3)]
                samples.append((optical, emitted))
            (o0, e0), (o1, e1) = samples
            t0 = jnp.exp(-o0)
            for ch in range(3):
                out_ref[ch, rows, col] = e0[ch] + t0 * e1[ch]
            out_ref[3, rows, col] = jnp.exp(-(o0 + o1))
        return carry

    lax.fori_loop(0, groups, group_body, 0)


def render(density, bins, table, x_prev, x_next, h_top, h_bot, depth_scale):
    planes, rows, cols = density.shape
    n_blocks = rows // ROW_BLOCK
    eights = ROW_BLOCK // 8
    last8 = rows // 8 - 1
    blk3 = lambda r: (0, r, 0)
    return pl.pallas_call(
        functools.partial(render_kernel, depth_scale),
        grid=(n_blocks,),
        in_specs=[
            pl.BlockSpec((8, 2 * LANES), lambda r: (0, 0)),
            pl.BlockSpec((planes, ROW_BLOCK, cols), blk3),
            pl.BlockSpec((planes, 8, cols), lambda r: (0, jnp.maximum(r * eights - 1, 0), 0)),
            pl.BlockSpec((planes, 8, cols), lambda r: (0, jnp.minimum((r + 1) * eights, last8), 0)),
            pl.BlockSpec((planes, 8, cols), lambda r: (0, 0, 0)),
            pl.BlockSpec((planes, 8, cols), lambda r: (0, 0, 0)),
            pl.BlockSpec((ROW_BLOCK, cols), lambda r: (r, 0)),
            pl.BlockSpec((ROW_BLOCK, cols), lambda r: (r, 0)),
            pl.BlockSpec((planes, ROW_BLOCK, cols), blk3),
        ],
        out_specs=pl.BlockSpec((4, ROW_BLOCK, cols), blk3),
        out_shape=jax.ShapeDtypeStruct((4, rows, cols), jnp.float32),
    )(table, density, density, density, h_top, h_bot, x_prev, x_next, bins)


def per_device(density, bins, colors, extinction):
    depth_cells, row_cells, col_cells = density.shape
    slab_count = lax.axis_size("depth")
    tile_count = lax.axis_size("tile")
    depth_scale = 0.6 / (depth_cells * slab_count)
    fwd_d, bwd_d = shift_pair("depth", slab_count)
    fwd_t, bwd_t = shift_pair("tile", tile_count)
    x_prev = lax.ppermute(density[-1], "depth", fwd_d)
    x_next = lax.ppermute(density[0], "depth", bwd_d)
    h_top = lax.ppermute(density[:, row_cells - 8:], "tile", fwd_t)
    h_bot = lax.ppermute(density[:, :8], "tile", bwd_t)
    lookup = jnp.concatenate([colors, extinction[None, :]], 0).astype(jnp.float32)
    table = jnp.concatenate([lookup, jnp.zeros((4, lookup.shape[1]), jnp.float32)], 0)
    image_part = render(density, bins, table, x_prev, x_next, h_top, h_bot, depth_scale)
    slab_index = lax.axis_index("depth")
    for round_index in range(slab_count.bit_length() - 1):
        half_width = image_part.shape[2] // 2
        lower_part = image_part[:, :, :half_width]
        upper_part = image_part[:, :, half_width:]
        behind = jnp.right_shift(slab_index, round_index) % 2 == 1
        kept_part = jnp.where(behind, upper_part, lower_part)
        sent_part = jnp.where(behind, lower_part, upper_part)
        received = partner(sent_part, "depth", round_index)
        front = jnp.where(behind, received, kept_part)
        back = jnp.where(behind, kept_part, received)
        image_part = over_pair(front, back)
    return jnp.concatenate([image_part[:3], 1.0 - image_part[3:]], 0)


def solution(mesh):
    return jax.shard_map(
        per_device,
        mesh=mesh,
        in_specs=(P("depth", "tile", None), P("depth", "tile", None), P(), P()),
        out_specs=P(None, "tile", "depth"),
        check_vma=False,
    )
```

```python
import functools

import jax
import jax.numpy as jnp
from jax import lax
from jax.experimental import pallas as pl
from jax.experimental.pallas import tpu as pltpu
from jax.sharding import PartitionSpec as P

ROW_BLOCK = 32
LANES = 128


def shift_pair(axis, count):
    return [(i, i + 1) for i in range(count - 1)], [(i + 1, i) for i in range(count - 1)]


def partner(value, axis, stride):
    return lax.ppermute(value, axis, [(i, i ^ 1 << stride) for i in range(lax.axis_size(axis))])


def over_pair(front, back):
    return jnp.concatenate([front[:3] + front[3:] * back[:3], front[3:] * back[3:]], 0)


def render_kernel(depth_scale, table_ref, d_ref, dprev_ref, dnext_ref, htop_ref, hbot_ref,
                  xp_ref, xn_ref, b_ref, out_ref):
    block = pl.program_id(0)
    last_block = pl.num_programs(0) - 1
    chunks = d_ref.shape[1] // 8
    groups = d_ref.shape[2] // LANES
    sub = lax.broadcasted_iota(jnp.int32, (8, LANES), 0)
    lane = lax.broadcasted_iota(jnp.int32, (8, LANES), 1)
    tables = [
        (jnp.broadcast_to(table_ref[ch:ch + 1, 0:LANES], (8, LANES)),
         jnp.broadcast_to(table_ref[ch:ch + 1, LANES:2 * LANES], (8, LANES)))
        for ch in range(4)
    ]

    def look(idx):
        low = idx & (LANES - 1)
        high = idx >= LANES
        vals = []
        for lo_t, hi_t in tables:
            lo_v = jnp.take_along_axis(lo_t, low, axis=1, mode="promise_in_bounds")
            hi_v = jnp.take_along_axis(hi_t, low, axis=1, mode="promise_in_bounds")
            vals.append(jnp.where(high, hi_v, lo_v))
        return vals

    def group_body(g, carry):
        col = pl.ds(pl.multiple_of(g * LANES, LANES), LANES)
        col_l = pl.ds(pl.multiple_of(jnp.maximum(g - 1, 0) * LANES, LANES), LANES)
        col_r = pl.ds(pl.multiple_of(jnp.minimum(g + 1, groups - 1) * LANES, LANES), LANES)
        has_l = g > 0
        has_r = g < groups - 1
        centers = [[d_ref[p, pl.ds(k * 8, 8), col] for k in range(chunks)] for p in range(2)]
        for k in range(chunks):
            rows = pl.ds(k * 8, 8)
            samples = []
            for p in range(2):
                c = centers[p][k]
                if k == 0:
                    up_src = jnp.where(block == 0, htop_ref[p, :, col], dprev_ref[p, :, col])
                else:
                    up_src = centers[p][k - 1]
                if k == chunks - 1:
                    dn_src = jnp.where(block == last_block, hbot_ref[p, :, col], dnext_ref[p, :, col])
                else:
                    dn_src = centers[p][k + 1]
                up = jnp.where(sub == 0, pltpu.roll(up_src, 1, 0), pltpu.roll(c, 1, 0))
                dn = jnp.where(sub == 7, pltpu.roll(dn_src, 7, 0), pltpu.roll(c, 7, 0))
                grad_y = (dn - up) * 0.5
                left_src = jnp.where(has_l, d_ref[p, rows, col_l], 0.0)
                right_src = jnp.where(has_r, d_ref[p, rows, col_r], 0.0)
                lf = jnp.where(lane == 0, pltpu.roll(left_src, 1, 1), pltpu.roll(c, 1, 1))
                rt = jnp.where(lane == LANES - 1, pltpu.roll(right_src, LANES - 1, 1),
                               pltpu.roll(c, LANES - 1, 1))
                grad_z = (rt - lf) * 0.5
                if p == 0:
                    grad_x = (centers[1][k] - xp_ref[rows, col]) * 0.5
                else:
                    grad_x = (xn_ref[rows, col] - centers[0][k]) * 0.5
                lit = jnp.abs(0.48 * grad_x + 0.6 * grad_y + 0.64 * grad_z)
                shade = 0.3 + 0.7 * lit / jnp.sqrt(
                    grad_x * grad_x + grad_y * grad_y + grad_z * grad_z + 1.0)
                entries = look(b_ref[p, rows, col])
                optical = entries[3] * depth_scale
                absorb = 1.0 - jnp.exp(-optical)
                emitted = [entries[ch] * shade * absorb for ch in range(3)]
                samples.append((optical, emitted))
            (o0, e0), (o1, e1) = samples
            t0 = jnp.exp(-o0)
            for ch in range(3):
                out_ref[ch, rows, col] = e0[ch] + t0 * e1[ch]
            out_ref[3, rows, col] = jnp.exp(-(o0 + o1))
        return carry

    lax.fori_loop(0, groups, group_body, 0)


def render(density, bins, table, x_prev, x_next, h_top, h_bot, depth_scale):
    planes, rows, cols = density.shape
    n_blocks = rows // ROW_BLOCK
    eights = ROW_BLOCK // 8
    last8 = rows // 8 - 1
    blk3 = lambda r: (0, r, 0)
    return pl.pallas_call(
        functools.partial(render_kernel, depth_scale),
        grid=(n_blocks,),
        in_specs=[
            pl.BlockSpec((8, 2 * LANES), lambda r: (0, 0)),
            pl.BlockSpec((planes, ROW_BLOCK, cols), blk3),
            pl.BlockSpec((planes, 8, cols), lambda r: (0, jnp.maximum(r * eights - 1, 0), 0)),
            pl.BlockSpec((planes, 8, cols), lambda r: (0, jnp.minimum((r + 1) * eights, last8), 0)),
            pl.BlockSpec((planes, 8, cols), lambda r: (0, 0, 0)),
            pl.BlockSpec((planes, 8, cols), lambda r: (0, 0, 0)),
            pl.BlockSpec((ROW_BLOCK, cols), lambda r: (r, 0)),
            pl.BlockSpec((ROW_BLOCK, cols), lambda r: (r, 0)),
            pl.BlockSpec((planes, ROW_BLOCK, cols), blk3),
        ],
        out_specs=pl.BlockSpec((4, ROW_BLOCK, cols), blk3),
        out_shape=jax.ShapeDtypeStruct((4, rows, cols), jnp.float32),
    )(table, density, density, density, h_top, h_bot, x_prev, x_next, bins)


def combine_into(dst_ref, kept_ref, kept_off, rcv_ref, behind, rows, width, lane_axis, finish=False):
    chunk_rows = 8
    lanes = min(width, LANES) if lane_axis else LANES
    groups = width // lanes if lane_axis else 1

    def body(i, carry):
        for j in range(groups):
            if lane_axis:
                r_sl = pl.ds(pl.multiple_of(i * chunk_rows, chunk_rows), chunk_rows)
                k_sl = (r_sl, pl.ds(pl.multiple_of(kept_off + j * lanes, lanes), lanes))
                d_sl = (r_sl, pl.ds(j * lanes, lanes))
            else:
                r_k = pl.ds(pl.multiple_of(kept_off + i * chunk_rows, chunk_rows), chunk_rows)
                r_d = pl.ds(pl.multiple_of(i * chunk_rows, chunk_rows), chunk_rows)
                k_sl = (r_k, slice(None))
                d_sl = (r_d, slice(None))
            kept = [kept_ref[(ch,) + k_sl] for ch in range(4)]
            rcv = [rcv_ref[(ch,) + d_sl] for ch in range(4)]
            front = [jnp.where(behind, b, a) for a, b in zip(kept, rcv)]
            back = [jnp.where(behind, a, b) for a, b in zip(kept, rcv)]
            for ch in range(3):
                dst_ref[(ch,) + d_sl] = front[ch] + front[3] * back[ch]
            trans = front[3] * back[3]
            dst_ref[(3,) + d_sl] = (1.0 - trans) if finish else trans
        return carry

    lax.fori_loop(0, rows // chunk_rows, body, 0)


def composite_kernel(n_rounds, lane_rounds, img_ref, out_ref, *scratch):
    recv = scratch[:n_rounds]
    acc = scratch[n_rounds:2 * n_rounds - 1]
    flip_ref = scratch[2 * n_rounds - 1]
    send_sems, recv_sems = scratch[2 * n_rounds:]
    me = lax.axis_index("depth")
    tile = lax.axis_index("tile")
    bits = [(me // (1 << r)) % 2 for r in range(n_rounds)]
    partners = [me + (1 - 2 * bits[r]) * (1 << r) for r in range(n_rounds)]

    barrier = pltpu.get_barrier_semaphore()
    for r in range(n_rounds):
        pl.semaphore_signal(barrier, inc=1, device_id=(partners[r], tile),
                            device_id_type=pl.DeviceIdType.MESH)
    pl.semaphore_wait(barrier, n_rounds)

    rows = img_ref.shape[1]
    width = img_ref.shape[2]
    src = img_ref
    for r in range(n_rounds):
        half = width >> (r + 1)
        behind = bits[r] == 1
        send_off = (1 - bits[r]) * half
        keep_off = bits[r] * half
        lane_axis = r < lane_rounds
        if r == lane_rounds:
            for ch in range(4):
                flip_ref[ch] = src[ch].T
            src = flip_ref
        if lane_axis:
            src_view = src.at[:, :, pl.ds(pl.multiple_of(send_off, LANES), half)]
        else:
            src_view = src.at[:, pl.ds(pl.multiple_of(send_off, 8), half), :]
        copy = pltpu.make_async_remote_copy(
            src_ref=src_view,
            dst_ref=recv[r],
            send_sem=send_sems.at[r],
            recv_sem=recv_sems.at[r],
            device_id=(partners[r], tile),
            device_id_type=pl.DeviceIdType.MESH,
        )
        copy.start()
        copy.wait()
        last = r == n_rounds - 1
        dst = out_ref if last else acc[r]
        if lane_axis:
            combine_into(dst, src, keep_off, recv[r], behind, rows, half, True)
        else:
            combine_into(dst, src, keep_off, recv[r], behind, half, rows, False, finish=last)
        src = dst


def composite(image_part, n_rounds):
    chans, rows, width = image_part.shape
    lane_rounds = 0
    while (width >> (lane_rounds + 1)) >= LANES and lane_rounds < n_rounds:
        lane_rounds += 1
    recv_shapes = []
    for r in range(n_rounds):
        half = width >> (r + 1)
        recv_shapes.append((chans, rows, half) if r < lane_rounds else (chans, half, rows))
    final = recv_shapes[-1]
    scratch = [pltpu.VMEM(s, jnp.float32) for s in recv_shapes]
    scratch += [pltpu.VMEM(s, jnp.float32) for s in recv_shapes[:-1]]
    scratch += [pltpu.VMEM((chans, width >> lane_rounds, rows), jnp.float32)]
    scratch += [pltpu.SemaphoreType.DMA((n_rounds,)), pltpu.SemaphoreType.DMA((n_rounds,))]
    out = pl.pallas_call(
        functools.partial(composite_kernel, n_rounds, lane_rounds),
        out_shape=jax.ShapeDtypeStruct(final, jnp.float32),
        in_specs=[pl.BlockSpec(memory_space=pltpu.VMEM)],
        out_specs=pl.BlockSpec(memory_space=pltpu.VMEM),
        scratch_shapes=scratch,
        compiler_params=pltpu.CompilerParams(
            collective_id=0, has_side_effects=True, vmem_limit_bytes=48 * 1024 * 1024),
    )(image_part)
    return jnp.transpose(out, (0, 2, 1))


def per_device(density, bins, colors, extinction):
    depth_cells, row_cells, col_cells = density.shape
    slab_count = lax.axis_size("depth")
    tile_count = lax.axis_size("tile")
    depth_scale = 0.6 / (depth_cells * slab_count)
    fwd_d, bwd_d = shift_pair("depth", slab_count)
    fwd_t, bwd_t = shift_pair("tile", tile_count)
    x_prev = lax.ppermute(density[-1], "depth", fwd_d)
    x_next = lax.ppermute(density[0], "depth", bwd_d)
    h_top = lax.ppermute(density[:, row_cells - 8:], "tile", fwd_t)
    h_bot = lax.ppermute(density[:, :8], "tile", bwd_t)
    lookup = jnp.concatenate([colors, extinction[None, :]], 0).astype(jnp.float32)
    table = jnp.concatenate([lookup, jnp.zeros((4, lookup.shape[1]), jnp.float32)], 0)
    image_part = render(density, bins, table, x_prev, x_next, h_top, h_bot, depth_scale)
    return composite(image_part, slab_count.bit_length() - 1)


def solution(mesh):
    return jax.shard_map(
        per_device,
        mesh=mesh,
        in_specs=(P("depth", "tile", None), P("depth", "tile", None), P(), P()),
        out_specs=P(None, "tile", "depth"),
        check_vma=False,
    )
```

```python
import functools

import jax
import jax.numpy as jnp
from jax import lax
from jax.experimental import pallas as pl
from jax.experimental.pallas import tpu as pltpu
from jax.sharding import PartitionSpec as P

ROW_BLOCK = 32
LANES = 128


def shift_pair(axis, count):
    return [(i, i + 1) for i in range(count - 1)], [(i + 1, i) for i in range(count - 1)]


def render_rows(depth_scale, tables, c, n_chunks, d_ref, htop_ref, hbot_ref, xp_ref, xn_ref, b_ref,
                img_ref):
    row_block = d_ref.shape[1] // n_chunks
    chunks = row_block // 8
    groups = d_ref.shape[2] // LANES
    base = c * row_block
    sub = lax.broadcasted_iota(jnp.int32, (8, LANES), 0)
    lane = lax.broadcasted_iota(jnp.int32, (8, LANES), 1)

    def look(idx):
        low = idx & (LANES - 1)
        high = idx >= LANES
        vals = []
        for lo_t, hi_t in tables:
            lo_v = jnp.take_along_axis(lo_t, low, axis=1, mode="promise_in_bounds")
            hi_v = jnp.take_along_axis(hi_t, low, axis=1, mode="promise_in_bounds")
            vals.append(jnp.where(high, hi_v, lo_v))
        return vals

    def group_body(g, carry):
        col = pl.ds(pl.multiple_of(g * LANES, LANES), LANES)
        col_l = pl.ds(pl.multiple_of(jnp.maximum(g - 1, 0) * LANES, LANES), LANES)
        col_r = pl.ds(pl.multiple_of(jnp.minimum(g + 1, groups - 1) * LANES, LANES), LANES)
        has_l = g > 0
        has_r = g < groups - 1
        centers = [[d_ref[p, pl.ds(base + k * 8, 8), col] for k in range(chunks)] for p in range(2)]
        for k in range(chunks):
            rows = pl.ds(base + k * 8, 8)
            samples = []
            for p in range(2):
                c_v = centers[p][k]
                if k > 0:
                    up_src = centers[p][k - 1]
                elif c == 0:
                    up_src = htop_ref[p, :, col]
                else:
                    up_src = d_ref[p, pl.ds(base - 8, 8), col]
                if k < chunks - 1:
                    dn_src = centers[p][k + 1]
                elif c == n_chunks - 1:
                    dn_src = hbot_ref[p, :, col]
                else:
                    dn_src = d_ref[p, pl.ds(base + row_block, 8), col]
                up = jnp.where(sub == 0, pltpu.roll(up_src, 1, 0), pltpu.roll(c_v, 1, 0))
                dn = jnp.where(sub == 7, pltpu.roll(dn_src, 7, 0), pltpu.roll(c_v, 7, 0))
                grad_y = (dn - up) * 0.5
                left_src = jnp.where(has_l, d_ref[p, rows, col_l], 0.0)
                right_src = jnp.where(has_r, d_ref[p, rows, col_r], 0.0)
                lf = jnp.where(lane == 0, pltpu.roll(left_src, 1, 1), pltpu.roll(c_v, 1, 1))
                rt = jnp.where(lane == LANES - 1, pltpu.roll(right_src, LANES - 1, 1),
                               pltpu.roll(c_v, LANES - 1, 1))
                grad_z = (rt - lf) * 0.5
                if p == 0:
                    grad_x = (centers[1][k] - xp_ref[rows, col]) * 0.5
                else:
                    grad_x = (xn_ref[rows, col] - centers[0][k]) * 0.5
                lit = jnp.abs(0.48 * grad_x + 0.6 * grad_y + 0.64 * grad_z)
                shade = 0.3 + 0.7 * lit / jnp.sqrt(
                    grad_x * grad_x + grad_y * grad_y + grad_z * grad_z + 1.0)
                entries = look(b_ref[p, rows, col])
                optical = entries[3] * depth_scale
                absorb = 1.0 - jnp.exp(-optical)
                emitted = [entries[ch] * shade * absorb for ch in range(3)]
                samples.append((optical, emitted))
            (o0, e0), (o1, e1) = samples
            t0 = jnp.exp(-o0)
            for ch in range(3):
                img_ref[ch, rows, col] = e0[ch] + t0 * e1[ch]
            img_ref[3, rows, col] = jnp.exp(-(o0 + o1))
        return carry

    lax.fori_loop(0, groups, group_body, 0)


def combine_lanes(dst_ref, src_ref, keep_off, rcv_ref, behind, row0, n_rows, half):
    lanes = min(half, LANES)
    groups = half // lanes

    def body(i, carry):
        r_sl = pl.ds(pl.multiple_of(row0 + i * 8, 8), 8)
        for j in range(groups):
            k_sl = pl.ds(pl.multiple_of(keep_off + j * lanes, lanes), lanes)
            d_sl = pl.ds(j * lanes, lanes)
            kept = [src_ref[ch, r_sl, k_sl] for ch in range(4)]
            rcv = [rcv_ref[ch, r_sl, d_sl] for ch in range(4)]
            front = [jnp.where(behind, q, k) for k, q in zip(kept, rcv)]
            back = [jnp.where(behind, k, q) for k, q in zip(kept, rcv)]
            for ch in range(3):
                dst_ref[ch, r_sl, d_sl] = front[ch] + front[3] * back[ch]
            dst_ref[3, r_sl, d_sl] = front[3] * back[3]
        return carry

    lax.fori_loop(0, n_rows // 8, body, 0)


def combine_rows(dst_ref, src_ref, keep_off, rcv_ref, behind, half, finish):
    def body(i, carry):
        r_k = pl.ds(pl.multiple_of(keep_off + i * 8, 8), 8)
        r_d = pl.ds(pl.multiple_of(i * 8, 8), 8)
        kept = [src_ref[ch, r_k, :] for ch in range(4)]
        rcv = [rcv_ref[ch, r_d, :] for ch in range(4)]
        front = [jnp.where(behind, q, k) for k, q in zip(kept, rcv)]
        back = [jnp.where(behind, k, q) for k, q in zip(kept, rcv)]
        for ch in range(3):
            dst_ref[ch, r_d, :] = front[ch] + front[3] * back[ch]
        trans = front[3] * back[3]
        dst_ref[3, r_d, :] = (1.0 - trans) if finish else trans
        return carry

    lax.fori_loop(0, half // 8, body, 0)


def fused_kernel(depth_scale, n_rounds, lane_rounds, n_chunks, table_ref, d_ref, htop_ref, hbot_ref,
                 xp_ref, xn_ref, b_ref, out_ref, img_ref, *scratch):
    recv = scratch[:n_rounds]
    acc = scratch[n_rounds:2 * n_rounds - 1]
    flip_ref = scratch[2 * n_rounds - 1]
    send_sems, recv_sems = scratch[2 * n_rounds:]
    me = lax.axis_index("depth")
    tile = lax.axis_index("tile")
    bits = [(me // (1 << r)) % 2 for r in range(n_rounds)]
    partners = [me + (1 - 2 * bits[r]) * (1 << r) for r in range(n_rounds)]
    rows = d_ref.shape[1]
    width = d_ref.shape[2]
    row_block = rows // n_chunks
    halves = [width >> (r + 1) for r in range(n_rounds)]
    srcs = [img_ref] + list(acc)

    barrier = pltpu.get_barrier_semaphore()
    for r in range(n_rounds):
        pl.semaphore_signal(barrier, inc=1, device_id=(partners[r], tile),
                            device_id_type=pl.DeviceIdType.MESH)
    pl.semaphore_wait(barrier, n_rounds)

    tables = [
        (jnp.broadcast_to(table_ref[ch:ch + 1, 0:LANES], (8, LANES)),
         jnp.broadcast_to(table_ref[ch:ch + 1, LANES:2 * LANES], (8, LANES)))
        for ch in range(4)
    ]
    copies = {}

    def start_lane(r, c):
        row_sl = pl.ds(c * row_block, row_block)
        send_off = pl.multiple_of((1 - bits[r]) * halves[r], LANES)
        copy = pltpu.make_async_remote_copy(
            src_ref=srcs[r].at[:, row_sl, pl.ds(send_off, halves[r])],
            dst_ref=recv[r].at[:, row_sl, :],
            send_sem=send_sems.at[r * n_chunks + c],
            recv_sem=recv_sems.at[r * n_chunks + c],
            device_id=(partners[r], tile),
            device_id_type=pl.DeviceIdType.MESH,
        )
        copy.start()
        copies[(r, c)] = copy

    def finish_lane(r, c):
        copies[(r, c)].wait()
        combine_lanes(acc[r], srcs[r], bits[r] * halves[r], recv[r], bits[r] == 1,
                      c * row_block, row_block, halves[r])
        if r + 1 < lane_rounds:
            start_lane(r + 1, c)

    for c in range(n_chunks):
        render_rows(depth_scale, tables, c, n_chunks, d_ref, htop_ref, hbot_ref, xp_ref, xn_ref,
                    b_ref, img_ref)
        start_lane(0, c)
        if c >= 1:
            finish_lane(0, c - 1)
    finish_lane(0, n_chunks - 1)
    for r in range(1, lane_rounds):
        for c in range(n_chunks):
            finish_lane(r, c)

    src = acc[lane_rounds - 1]
    for ch in range(4):
        flip_ref[ch] = src[ch].T
    src = flip_ref
    sem_base = lane_rounds * n_chunks
    for r in range(lane_rounds, n_rounds):
        half = halves[r]
        send_off = pl.multiple_of((1 - bits[r]) * half, 8)
        copy = pltpu.make_async_remote_copy(
            src_ref=src.at[:, pl.ds(send_off, half), :],
            dst_ref=recv[r],
            send_sem=send_sems.at[sem_base + r - lane_rounds],
            recv_sem=recv_sems.at[sem_base + r - lane_rounds],
            device_id=(partners[r], tile),
            device_id_type=pl.DeviceIdType.MESH,
        )
        copy.start()
        copy.wait()
        last = r == n_rounds - 1
        dst = out_ref if last else acc[r]
        combine_rows(dst, src, bits[r] * half, recv[r], bits[r] == 1, half, last)
        src = dst


def render_composite(density, bins, table, x_prev, x_next, h_top, h_bot, depth_scale, n_rounds):
    planes, rows, width = density.shape
    lane_rounds = 0
    while (width >> (lane_rounds + 1)) >= LANES and lane_rounds < n_rounds:
        lane_rounds += 1
    n_chunks = rows // ROW_BLOCK
    shapes = []
    for r in range(n_rounds):
        half = width >> (r + 1)
        shapes.append((4, rows, half) if r < lane_rounds else (4, half, rows))
    scratch = [pltpu.VMEM((4, rows, width), jnp.float32)]
    scratch += [pltpu.VMEM(s, jnp.float32) for s in shapes]
    scratch += [pltpu.VMEM(s, jnp.float32) for s in shapes[:-1]]
    scratch += [pltpu.VMEM((4, width >> lane_rounds, rows), jnp.float32)]
    n_sems = lane_rounds * n_chunks + n_rounds - lane_rounds
    scratch += [pltpu.SemaphoreType.DMA((n_sems,)), pltpu.SemaphoreType.DMA((n_sems,))]
    vmem = pl.BlockSpec(memory_space=pltpu.VMEM)
    out = pl.pallas_call(
        functools.partial(fused_kernel, depth_scale, n_rounds, lane_rounds, n_chunks),
        out_shape=jax.ShapeDtypeStruct(shapes[-1], jnp.float32),
        in_specs=[vmem] * 7,
        out_specs=vmem,
        scratch_shapes=scratch,
        compiler_params=pltpu.CompilerParams(
            collective_id=0, has_side_effects=True, vmem_limit_bytes=60 * 1024 * 1024),
    )(table, density, h_top, h_bot, x_prev, x_next, bins)
    return jnp.transpose(out, (0, 2, 1))


def per_device(density, bins, colors, extinction):
    depth_cells, row_cells, col_cells = density.shape
    slab_count = lax.axis_size("depth")
    tile_count = lax.axis_size("tile")
    depth_scale = 0.6 / (depth_cells * slab_count)
    fwd_d, bwd_d = shift_pair("depth", slab_count)
    fwd_t, bwd_t = shift_pair("tile", tile_count)
    x_prev = lax.ppermute(density[-1], "depth", fwd_d)
    x_next = lax.ppermute(density[0], "depth", bwd_d)
    h_top = lax.ppermute(density[:, row_cells - 8:], "tile", fwd_t)
    h_bot = lax.ppermute(density[:, :8], "tile", bwd_t)
    lookup = jnp.concatenate([colors, extinction[None, :]], 0).astype(jnp.float32)
    table = jnp.concatenate([lookup, jnp.zeros((4, lookup.shape[1]), jnp.float32)], 0)
    return render_composite(density, bins, table, x_prev, x_next, h_top, h_bot, depth_scale,
                            slab_count.bit_length() - 1)


def solution(mesh):
    return jax.shard_map(
        per_device,
        mesh=mesh,
        in_specs=(P("depth", "tile", None), P("depth", "tile", None), P(), P()),
        out_specs=P(None, "tile", "depth"),
        check_vma=False,
    )
```

```python
import functools

import jax
import jax.numpy as jnp
from jax import lax
from jax.experimental import pallas as pl
from jax.experimental.pallas import tpu as pltpu
from jax.sharding import PartitionSpec as P

ROW_BLOCK = 32
LANES = 128


def make_look(tables):
    def look(idx):
        low = idx & (LANES - 1)
        high = idx >= LANES
        vals = []
        for lo_t, hi_t in tables:
            lo_v = jnp.take_along_axis(lo_t, low, axis=1, mode="promise_in_bounds")
            hi_v = jnp.take_along_axis(hi_t, low, axis=1, mode="promise_in_bounds")
            vals.append(jnp.where(high, hi_v, lo_v))
        return vals

    return look


def lookup_rows(depth_scale, look, b_ref, stash_ref, img_ref):
    rows = b_ref.shape[1]
    groups = b_ref.shape[2] // LANES

    def body(i, carry):
        g = i % groups
        k = i // groups
        col = pl.ds(pl.multiple_of(g * LANES, LANES), LANES)
        r_sl = pl.ds(pl.multiple_of(k * 8, 8), 8)
        e0 = look(b_ref[0, r_sl, col])
        e1 = look(b_ref[1, r_sl, col])
        o0 = e0[3] * depth_scale
        o1 = e1[3] * depth_scale
        a0 = 1.0 - jnp.exp(-o0)
        a1 = 1.0 - jnp.exp(-o1)
        t0 = jnp.exp(-o0)
        for ch in range(3):
            stash_ref[ch, r_sl, col] = e0[ch] * a0
            stash_ref[3 + ch, r_sl, col] = t0 * (e1[ch] * a1)
        img_ref[3, r_sl, col] = jnp.exp(-(o0 + o1))
        return carry

    lax.fori_loop(0, (rows // 8) * groups, body, 0)


def shade_rows(c, n_chunks, d_ref, htop_ref, hbot_ref, xp_ref, xn_ref, has_top, has_bot,
               has_prev, has_next, stash_ref, img_ref):
    row_block = d_ref.shape[1] // n_chunks
    chunks = row_block // 8
    groups = d_ref.shape[2] // LANES
    base = c * row_block
    sub = lax.broadcasted_iota(jnp.int32, (8, LANES), 0)
    lane = lax.broadcasted_iota(jnp.int32, (8, LANES), 1)

    def group_body(g, carry):
        col = pl.ds(pl.multiple_of(g * LANES, LANES), LANES)
        col_l = pl.ds(pl.multiple_of(jnp.maximum(g - 1, 0) * LANES, LANES), LANES)
        col_r = pl.ds(pl.multiple_of(jnp.minimum(g + 1, groups - 1) * LANES, LANES), LANES)
        has_l = g > 0
        has_r = g < groups - 1
        centers = [[d_ref[p, pl.ds(base + k * 8, 8), col] for k in range(chunks)] for p in range(2)]
        for k in range(chunks):
            rows = pl.ds(base + k * 8, 8)
            shades = []
            for p in range(2):
                c_v = centers[p][k]
                if k > 0:
                    up_src = centers[p][k - 1]
                elif c == 0:
                    up_src = jnp.where(has_top, htop_ref[p, :, col], 0.0)
                else:
                    up_src = d_ref[p, pl.ds(base - 8, 8), col]
                if k < chunks - 1:
                    dn_src = centers[p][k + 1]
                elif c == n_chunks - 1:
                    dn_src = jnp.where(has_bot, hbot_ref[p, :, col], 0.0)
                else:
                    dn_src = d_ref[p, pl.ds(base + row_block, 8), col]
                up = jnp.where(sub == 0, pltpu.roll(up_src, 1, 0), pltpu.roll(c_v, 1, 0))
                dn = jnp.where(sub == 7, pltpu.roll(dn_src, 7, 0), pltpu.roll(c_v, 7, 0))
                grad_y = (dn - up) * 0.5
                left_src = jnp.where(has_l, d_ref[p, rows, col_l], 0.0)
                right_src = jnp.where(has_r, d_ref[p, rows, col_r], 0.0)
                lf = jnp.where(lane == 0, pltpu.roll(left_src, 1, 1), pltpu.roll(c_v, 1, 1))
                rt = jnp.where(lane == LANES - 1, pltpu.roll(right_src, LANES - 1, 1),
                               pltpu.roll(c_v, LANES - 1, 1))
                grad_z = (rt - lf) * 0.5
                if p == 0:
                    grad_x = (centers[1][k] - jnp.where(has_prev, xp_ref[rows, col], 0.0)) * 0.5
                else:
                    grad_x = (jnp.where(has_next, xn_ref[rows, col], 0.0) - centers[0][k]) * 0.5
                lit = jnp.abs(0.48 * grad_x + 0.6 * grad_y + 0.64 * grad_z)
                shades.append(0.3 + 0.7 * lit / jnp.sqrt(
                    grad_x * grad_x + grad_y * grad_y + grad_z * grad_z + 1.0))
            for ch in range(3):
                img_ref[ch, rows, col] = (stash_ref[ch, rows, col] * shades[0]
                                          + stash_ref[3 + ch, rows, col] * shades[1])
        return carry

    lax.fori_loop(0, groups, group_body, 0)


def combine_lanes(dst_ref, src_ref, keep_off, rcv_ref, behind, row0, n_rows, half):
    lanes = min(half, LANES)
    groups = half // lanes

    def body(i, carry):
        r_sl = pl.ds(pl.multiple_of(row0 + i * 8, 8), 8)
        for j in range(groups):
            k_sl = pl.ds(pl.multiple_of(keep_off + j * lanes, lanes), lanes)
            d_sl = pl.ds(j * lanes, lanes)
            kept = [src_ref[ch, r_sl, k_sl] for ch in range(4)]
            rcv = [rcv_ref[ch, r_sl, d_sl] for ch in range(4)]
            front = [jnp.where(behind, q, k) for k, q in zip(kept, rcv)]
            back = [jnp.where(behind, k, q) for k, q in zip(kept, rcv)]
            for ch in range(3):
                dst_ref[ch, r_sl, d_sl] = front[ch] + front[3] * back[ch]
            dst_ref[3, r_sl, d_sl] = front[3] * back[3]
        return carry

    lax.fori_loop(0, n_rows // 8, body, 0)


def combine_rows(dst_ref, src_ref, keep_off, rcv_ref, behind, half, finish):
    def body(i, carry):
        r_k = pl.ds(pl.multiple_of(keep_off + i * 8, 8), 8)
        r_d = pl.ds(pl.multiple_of(i * 8, 8), 8)
        kept = [src_ref[ch, r_k, :] for ch in range(4)]
        rcv = [rcv_ref[ch, r_d, :] for ch in range(4)]
        front = [jnp.where(behind, q, k) for k, q in zip(kept, rcv)]
        back = [jnp.where(behind, k, q) for k, q in zip(kept, rcv)]
        for ch in range(3):
            dst_ref[ch, r_d, :] = front[ch] + front[3] * back[ch]
        trans = front[3] * back[3]
        dst_ref[3, r_d, :] = (1.0 - trans) if finish else trans
        return carry

    lax.fori_loop(0, half // 8, body, 0)


def fused_kernel(depth_scale, n_rounds, lane_rounds, n_chunks, table_ref, d_ref, b_ref, out_ref,
                 img_ref, stash_ref, xp_ref, xn_ref, htop_ref, hbot_ref, halo_send, halo_recv, *scratch):
    recv = scratch[:n_rounds]
    acc = scratch[n_rounds:2 * n_rounds - 1]
    flip_ref = scratch[2 * n_rounds - 1]
    send_sems, recv_sems = scratch[2 * n_rounds:]
    me = lax.axis_index("depth")
    tile = lax.axis_index("tile")
    n_slabs = lax.axis_size("depth")
    n_tiles = lax.axis_size("tile")
    bits = [(me // (1 << r)) % 2 for r in range(n_rounds)]
    partners = [me + (1 - 2 * bits[r]) * (1 << r) for r in range(n_rounds)]
    rows = d_ref.shape[1]
    width = d_ref.shape[2]
    row_block = rows // n_chunks
    halves = [width >> (r + 1) for r in range(n_rounds)]
    srcs = [img_ref] + list(acc)
    mesh_id = pl.DeviceIdType.MESH
    has_prev = me > 0
    has_next = me < n_slabs - 1
    has_top = tile > 0
    has_bot = tile < n_tiles - 1
    odd = bits[0] == 1
    extra_nb = jnp.where(odd, has_next, has_prev)
    extra_id = jnp.where(odd, me + 1, me - 1)

    barrier = pltpu.get_barrier_semaphore()
    for r in range(n_rounds):
        pl.semaphore_signal(barrier, inc=1, device_id=(partners[r], tile), device_id_type=mesh_id)

    @pl.when(extra_nb)
    def _():
        pl.semaphore_signal(barrier, inc=1, device_id=(extra_id, tile), device_id_type=mesh_id)

    @pl.when(has_top)
    def _():
        pl.semaphore_signal(barrier, inc=1, device_id=(me, tile - 1), device_id_type=mesh_id)

    @pl.when(has_bot)
    def _():
        pl.semaphore_signal(barrier, inc=1, device_id=(me, tile + 1), device_id_type=mesh_id)

    n_greet = (n_rounds + extra_nb.astype(jnp.int32) + has_top.astype(jnp.int32)
               + has_bot.astype(jnp.int32))
    pl.semaphore_wait(barrier, n_greet)

    halo_copies = [
        (has_next, has_prev, pltpu.make_async_remote_copy(
            src_ref=d_ref.at[1], dst_ref=xp_ref, send_sem=halo_send.at[0],
            recv_sem=halo_recv.at[0], device_id=(me + 1, tile), device_id_type=mesh_id)),
        (has_prev, has_next, pltpu.make_async_remote_copy(
            src_ref=d_ref.at[0], dst_ref=xn_ref, send_sem=halo_send.at[1],
            recv_sem=halo_recv.at[1], device_id=(me - 1, tile), device_id_type=mesh_id)),
        (has_bot, has_top, pltpu.make_async_remote_copy(
            src_ref=d_ref.at[:, pl.ds(rows - 8, 8), :], dst_ref=htop_ref, send_sem=halo_send.at[2],
            recv_sem=halo_recv.at[2], device_id=(me, tile + 1), device_id_type=mesh_id)),
        (has_top, has_bot, pltpu.make_async_remote_copy(
            src_ref=d_ref.at[:, pl.ds(0, 8), :], dst_ref=hbot_ref, send_sem=halo_send.at[3],
            recv_sem=halo_recv.at[3], device_id=(me, tile - 1), device_id_type=mesh_id)),
    ]
    for send_if, _, copy in halo_copies:
        pl.when(send_if)(copy.start)

    tables = [
        (jnp.broadcast_to(table_ref[ch:ch + 1, 0:LANES], (8, LANES)),
         jnp.broadcast_to(table_ref[ch:ch + 1, LANES:2 * LANES], (8, LANES)))
        for ch in range(4)
    ]
    lookup_rows(depth_scale, make_look(tables), b_ref, stash_ref, img_ref)
    for send_if, recv_if, copy in halo_copies:
        pl.when(send_if)(copy.wait_send)
        pl.when(recv_if)(copy.wait_recv)
    copies = {}

    def start_lane(r, c):
        row_sl = pl.ds(c * row_block, row_block)
        send_off = pl.multiple_of((1 - bits[r]) * halves[r], LANES)
        copy = pltpu.make_async_remote_copy(
            src_ref=srcs[r].at[:, row_sl, pl.ds(send_off, halves[r])],
            dst_ref=recv[r].at[:, row_sl, :],
            send_sem=send_sems.at[r * n_chunks + c],
            recv_sem=recv_sems.at[r * n_chunks + c],
            device_id=(partners[r], tile),
            device_id_type=pl.DeviceIdType.MESH,
        )
        copy.start()
        copies[(r, c)] = copy

    def finish_lane(r, c):
        copies[(r, c)].wait()
        combine_lanes(acc[r], srcs[r], bits[r] * halves[r], recv[r], bits[r] == 1,
                      c * row_block, row_block, halves[r])
        if r + 1 < lane_rounds:
            start_lane(r + 1, c)

    for c in range(n_chunks):
        shade_rows(c, n_chunks, d_ref, htop_ref, hbot_ref, xp_ref, xn_ref, has_top, has_bot,
                   has_prev, has_next, stash_ref, img_ref)
        start_lane(0, c)
        if c >= 1:
            finish_lane(0, c - 1)
    finish_lane(0, n_chunks - 1)
    for r in range(1, lane_rounds):
        for c in range(n_chunks):
            finish_lane(r, c)

    src = acc[lane_rounds - 1]
    for ch in range(4):
        flip_ref[ch] = src[ch].T
    src = flip_ref
    sem_base = lane_rounds * n_chunks
    for r in range(lane_rounds, n_rounds):
        half = halves[r]
        send_off = pl.multiple_of((1 - bits[r]) * half, 8)
        copy = pltpu.make_async_remote_copy(
            src_ref=src.at[:, pl.ds(send_off, half), :],
            dst_ref=recv[r],
            send_sem=send_sems.at[sem_base + r - lane_rounds],
            recv_sem=recv_sems.at[sem_base + r - lane_rounds],
            device_id=(partners[r], tile),
            device_id_type=pl.DeviceIdType.MESH,
        )
        copy.start()
        copy.wait()
        last = r == n_rounds - 1
        dst = out_ref if last else acc[r]
        combine_rows(dst, src, bits[r] * half, recv[r], bits[r] == 1, half, last)
        src = dst


def render_composite(density, bins, table, depth_scale, n_rounds):
    planes, rows, width = density.shape
    lane_rounds = 0
    while (width >> (lane_rounds + 1)) >= LANES and lane_rounds < n_rounds:
        lane_rounds += 1
    n_chunks = rows // ROW_BLOCK
    shapes = []
    for r in range(n_rounds):
        half = width >> (r + 1)
        shapes.append((4, rows, half) if r < lane_rounds else (4, half, rows))
    scratch = [
        pltpu.VMEM((4, rows, width), jnp.float32),
        pltpu.VMEM((6, rows, width), jnp.float32),
        pltpu.VMEM((rows, width), jnp.float32),
        pltpu.VMEM((rows, width), jnp.float32),
        pltpu.VMEM((planes, 8, width), jnp.float32),
        pltpu.VMEM((planes, 8, width), jnp.float32),
        pltpu.SemaphoreType.DMA((4,)),
        pltpu.SemaphoreType.DMA((4,)),
    ]
    scratch += [pltpu.VMEM(s, jnp.float32) for s in shapes]
    scratch += [pltpu.VMEM(s, jnp.float32) for s in shapes[:-1]]
    scratch += [pltpu.VMEM((4, width >> lane_rounds, rows), jnp.float32)]
    n_sems = lane_rounds * n_chunks + n_rounds - lane_rounds
    scratch += [pltpu.SemaphoreType.DMA((n_sems,)), pltpu.SemaphoreType.DMA((n_sems,))]
    vmem = pl.BlockSpec(memory_space=pltpu.VMEM)
    out = pl.pallas_call(
        functools.partial(fused_kernel, depth_scale, n_rounds, lane_rounds, n_chunks),
        out_shape=jax.ShapeDtypeStruct(shapes[-1], jnp.float32),
        in_specs=[vmem] * 3,
        out_specs=vmem,
        scratch_shapes=scratch,
        compiler_params=pltpu.CompilerParams(
            collective_id=0, has_side_effects=True, vmem_limit_bytes=48 * 1024 * 1024),
    )(table, density, bins)
    return jnp.transpose(out, (0, 2, 1))


def per_device(density, bins, colors, extinction):
    depth_cells = density.shape[0]
    slab_count = lax.axis_size("depth")
    depth_scale = 0.6 / (depth_cells * slab_count)
    lookup = jnp.concatenate([colors, extinction[None, :]], 0).astype(jnp.float32)
    table = jnp.concatenate([lookup, jnp.zeros((4, lookup.shape[1]), jnp.float32)], 0)
    return render_composite(density, bins, table, depth_scale, slab_count.bit_length() - 1)


def solution(mesh):
    return jax.shard_map(
        per_device,
        mesh=mesh,
        in_specs=(P("depth", "tile", None), P("depth", "tile", None), P(), P()),
        out_specs=P(None, "tile", "depth"),
        check_vma=False,
    )
```

```python
import functools

import jax
import jax.numpy as jnp
from jax import lax
from jax.experimental import pallas as pl
from jax.experimental.pallas import tpu as pltpu
from jax.sharding import PartitionSpec as P

ROW_BLOCK = 16
LANES = 128


def make_look(tables):
    def look(idx):
        low = idx & (LANES - 1)
        high = idx >= LANES
        vals = []
        for lo_t, hi_t in tables:
            lo_v = jnp.take_along_axis(lo_t, low, axis=1, mode="promise_in_bounds")
            hi_v = jnp.take_along_axis(hi_t, low, axis=1, mode="promise_in_bounds")
            vals.append(jnp.where(high, hi_v, lo_v))
        return vals

    return look


def lookup_rows(depth_scale, look, b_ref, stash_ref, img_ref):
    rows = b_ref.shape[1]
    groups = b_ref.shape[2] // LANES

    def body(i, carry):
        g = i % groups
        k = i // groups
        col = pl.ds(pl.multiple_of(g * LANES, LANES), LANES)
        r_sl = pl.ds(pl.multiple_of(k * 8, 8), 8)
        e0 = look(b_ref[0, r_sl, col])
        e1 = look(b_ref[1, r_sl, col])
        o0 = e0[3] * depth_scale
        o1 = e1[3] * depth_scale
        a0 = 1.0 - jnp.exp(-o0)
        a1 = 1.0 - jnp.exp(-o1)
        t0 = jnp.exp(-o0)
        for ch in range(3):
            stash_ref[ch, r_sl, col] = e0[ch] * a0
            stash_ref[3 + ch, r_sl, col] = t0 * (e1[ch] * a1)
        img_ref[3, r_sl, col] = jnp.exp(-(o0 + o1))
        return carry

    lax.fori_loop(0, (rows // 8) * groups, body, 0)


def shade_rows(c, n_chunks, d_ref, htop_ref, hbot_ref, xp_ref, xn_ref, has_top, has_bot,
               has_prev, has_next, stash_ref, img_ref):
    row_block = d_ref.shape[1] // n_chunks
    chunks = row_block // 8
    groups = d_ref.shape[2] // LANES
    base = c * row_block
    sub = lax.broadcasted_iota(jnp.int32, (8, LANES), 0)
    lane = lax.broadcasted_iota(jnp.int32, (8, LANES), 1)

    def group_body(g, carry):
        col = pl.ds(pl.multiple_of(g * LANES, LANES), LANES)
        col_l = pl.ds(pl.multiple_of(jnp.maximum(g - 1, 0) * LANES, LANES), LANES)
        col_r = pl.ds(pl.multiple_of(jnp.minimum(g + 1, groups - 1) * LANES, LANES), LANES)
        has_l = g > 0
        has_r = g < groups - 1
        centers = [[d_ref[p, pl.ds(base + k * 8, 8), col] for k in range(chunks)] for p in range(2)]
        for k in range(chunks):
            rows = pl.ds(base + k * 8, 8)
            shades = []
            for p in range(2):
                c_v = centers[p][k]
                if k > 0:
                    up_src = centers[p][k - 1]
                elif c == 0:
                    up_src = jnp.where(has_top, htop_ref[p, :, col], 0.0)
                else:
                    up_src = d_ref[p, pl.ds(base - 8, 8), col]
                if k < chunks - 1:
                    dn_src = centers[p][k + 1]
                elif c == n_chunks - 1:
                    dn_src = jnp.where(has_bot, hbot_ref[p, :, col], 0.0)
                else:
                    dn_src = d_ref[p, pl.ds(base + row_block, 8), col]
                up = jnp.where(sub == 0, pltpu.roll(up_src, 1, 0), pltpu.roll(c_v, 1, 0))
                dn = jnp.where(sub == 7, pltpu.roll(dn_src, 7, 0), pltpu.roll(c_v, 7, 0))
                grad_y = (dn - up) * 0.5
                left_src = jnp.where(has_l, d_ref[p, rows, col_l], 0.0)
                right_src = jnp.where(has_r, d_ref[p, rows, col_r], 0.0)
                lf = jnp.where(lane == 0, pltpu.roll(left_src, 1, 1), pltpu.roll(c_v, 1, 1))
                rt = jnp.where(lane == LANES - 1, pltpu.roll(right_src, LANES - 1, 1),
                               pltpu.roll(c_v, LANES - 1, 1))
                grad_z = (rt - lf) * 0.5
                if p == 0:
                    grad_x = (centers[1][k] - jnp.where(has_prev, xp_ref[rows, col], 0.0)) * 0.5
                else:
                    grad_x = (jnp.where(has_next, xn_ref[rows, col], 0.0) - centers[0][k]) * 0.5
                lit = jnp.abs(0.48 * grad_x + 0.6 * grad_y + 0.64 * grad_z)
                shades.append(0.3 + 0.7 * lit / jnp.sqrt(
                    grad_x * grad_x + grad_y * grad_y + grad_z * grad_z + 1.0))
            for ch in range(3):
                img_ref[ch, rows, col] = (stash_ref[ch, rows, col] * shades[0]
                                          + stash_ref[3 + ch, rows, col] * shades[1])
        return carry

    lax.fori_loop(0, groups, group_body, 0)


def combine_lanes(dst_ref, src_ref, keep_off, rcv_ref, behind, row0, n_rows, half):
    lanes = min(half, LANES)
    groups = half // lanes

    def body(i, carry):
        r_sl = pl.ds(pl.multiple_of(row0 + i * 8, 8), 8)
        for j in range(groups):
            k_sl = pl.ds(pl.multiple_of(keep_off + j * lanes, lanes), lanes)
            d_sl = pl.ds(j * lanes, lanes)
            kept = [src_ref[ch, r_sl, k_sl] for ch in range(4)]
            rcv = [rcv_ref[ch, r_sl, d_sl] for ch in range(4)]
            front = [jnp.where(behind, q, k) for k, q in zip(kept, rcv)]
            back = [jnp.where(behind, k, q) for k, q in zip(kept, rcv)]
            for ch in range(3):
                dst_ref[ch, r_sl, d_sl] = front[ch] + front[3] * back[ch]
            dst_ref[3, r_sl, d_sl] = front[3] * back[3]
        return carry

    lax.fori_loop(0, n_rows // 8, body, 0)


def combine_rows(dst_ref, src_ref, keep_off, rcv_ref, behind, half, finish):
    def body(i, carry):
        r_k = pl.ds(pl.multiple_of(keep_off + i * 8, 8), 8)
        r_d = pl.ds(pl.multiple_of(i * 8, 8), 8)
        kept = [src_ref[ch, r_k, :] for ch in range(4)]
        rcv = [rcv_ref[ch, r_d, :] for ch in range(4)]
        front = [jnp.where(behind, q, k) for k, q in zip(kept, rcv)]
        back = [jnp.where(behind, k, q) for k, q in zip(kept, rcv)]
        for ch in range(3):
            dst_ref[ch, r_d, :] = front[ch] + front[3] * back[ch]
        trans = front[3] * back[3]
        dst_ref[3, r_d, :] = (1.0 - trans) if finish else trans
        return carry

    lax.fori_loop(0, half // 8, body, 0)


def fused_kernel(depth_scale, n_rounds, lane_rounds, n_chunks, table_ref, d_ref, b_ref, out_ref,
                 img_ref, stash_ref, xp_ref, xn_ref, htop_ref, hbot_ref, halo_send, halo_recv, *scratch):
    recv = scratch[:n_rounds]
    acc = scratch[n_rounds:2 * n_rounds - 1]
    flip_ref = scratch[2 * n_rounds - 1]
    send_sems, recv_sems = scratch[2 * n_rounds:]
    me = lax.axis_index("depth")
    tile = lax.axis_index("tile")
    n_slabs = lax.axis_size("depth")
    n_tiles = lax.axis_size("tile")
    bits = [(me // (1 << r)) % 2 for r in range(n_rounds)]
    partners = [me + (1 - 2 * bits[r]) * (1 << r) for r in range(n_rounds)]
    rows = d_ref.shape[1]
    width = d_ref.shape[2]
    row_block = rows // n_chunks
    halves = [width >> (r + 1) for r in range(n_rounds)]
    srcs = [img_ref] + list(acc)
    mesh_id = pl.DeviceIdType.MESH
    has_prev = me > 0
    has_next = me < n_slabs - 1
    has_top = tile > 0
    has_bot = tile < n_tiles - 1
    odd = bits[0] == 1
    extra_nb = jnp.where(odd, has_next, has_prev)
    extra_id = jnp.where(odd, me + 1, me - 1)

    barrier = pltpu.get_barrier_semaphore()
    for r in range(n_rounds):
        pl.semaphore_signal(barrier, inc=1, device_id=(partners[r], tile), device_id_type=mesh_id)

    @pl.when(extra_nb)
    def _():
        pl.semaphore_signal(barrier, inc=1, device_id=(extra_id, tile), device_id_type=mesh_id)

    @pl.when(has_top)
    def _():
        pl.semaphore_signal(barrier, inc=1, device_id=(me, tile - 1), device_id_type=mesh_id)

    @pl.when(has_bot)
    def _():
        pl.semaphore_signal(barrier, inc=1, device_id=(me, tile + 1), device_id_type=mesh_id)

    n_greet = (n_rounds + extra_nb.astype(jnp.int32) + has_top.astype(jnp.int32)
               + has_bot.astype(jnp.int32))
    pl.semaphore_wait(barrier, n_greet)

    halo_copies = [
        (has_next, has_prev, pltpu.make_async_remote_copy(
            src_ref=d_ref.at[1], dst_ref=xp_ref, send_sem=halo_send.at[0],
            recv_sem=halo_recv.at[0], device_id=(me + 1, tile), device_id_type=mesh_id)),
        (has_prev, has_next, pltpu.make_async_remote_copy(
            src_ref=d_ref.at[0], dst_ref=xn_ref, send_sem=halo_send.at[1],
            recv_sem=halo_recv.at[1], device_id=(me - 1, tile), device_id_type=mesh_id)),
        (has_bot, has_top, pltpu.make_async_remote_copy(
            src_ref=d_ref.at[:, pl.ds(rows - 8, 8), :], dst_ref=htop_ref, send_sem=halo_send.at[2],
            recv_sem=halo_recv.at[2], device_id=(me, tile + 1), device_id_type=mesh_id)),
        (has_top, has_bot, pltpu.make_async_remote_copy(
            src_ref=d_ref.at[:, pl.ds(0, 8), :], dst_ref=hbot_ref, send_sem=halo_send.at[3],
            recv_sem=halo_recv.at[3], device_id=(me, tile - 1), device_id_type=mesh_id)),
    ]
    for send_if, _, copy in halo_copies:
        pl.when(send_if)(copy.start)

    tables = [
        (jnp.broadcast_to(table_ref[ch:ch + 1, 0:LANES], (8, LANES)),
         jnp.broadcast_to(table_ref[ch:ch + 1, LANES:2 * LANES], (8, LANES)))
        for ch in range(4)
    ]
    lookup_rows(depth_scale, make_look(tables), b_ref, stash_ref, img_ref)
    for send_if, recv_if, copy in halo_copies:
        pl.when(send_if)(copy.wait_send)
        pl.when(recv_if)(copy.wait_recv)
    copies = {}

    def start_lane(r, c):
        row_sl = pl.ds(c * row_block, row_block)
        send_off = pl.multiple_of((1 - bits[r]) * halves[r], LANES)
        copy = pltpu.make_async_remote_copy(
            src_ref=srcs[r].at[:, row_sl, pl.ds(send_off, halves[r])],
            dst_ref=recv[r].at[:, row_sl, :],
            send_sem=send_sems.at[r * n_chunks + c],
            recv_sem=recv_sems.at[r * n_chunks + c],
            device_id=(partners[r], tile),
            device_id_type=pl.DeviceIdType.MESH,
        )
        copy.start()
        copies[(r, c)] = copy

    def finish_lane(r, c):
        copies[(r, c)].wait()
        combine_lanes(acc[r], srcs[r], bits[r] * halves[r], recv[r], bits[r] == 1,
                      c * row_block, row_block, halves[r])
        if r + 1 < lane_rounds:
            start_lane(r + 1, c)

    for c in range(n_chunks):
        shade_rows(c, n_chunks, d_ref, htop_ref, hbot_ref, xp_ref, xn_ref, has_top, has_bot,
                   has_prev, has_next, stash_ref, img_ref)
        start_lane(0, c)
        if c >= 1:
            finish_lane(0, c - 1)
    finish_lane(0, n_chunks - 1)
    for r in range(1, lane_rounds):
        for c in range(n_chunks):
            finish_lane(r, c)

    src = acc[lane_rounds - 1]
    for ch in range(4):
        flip_ref[ch] = src[ch].T
    src = flip_ref
    sem_base = lane_rounds * n_chunks
    for r in range(lane_rounds, n_rounds):
        half = halves[r]
        send_off = pl.multiple_of((1 - bits[r]) * half, 8)
        copy = pltpu.make_async_remote_copy(
            src_ref=src.at[:, pl.ds(send_off, half), :],
            dst_ref=recv[r],
            send_sem=send_sems.at[sem_base + r - lane_rounds],
            recv_sem=recv_sems.at[sem_base + r - lane_rounds],
            device_id=(partners[r], tile),
            device_id_type=pl.DeviceIdType.MESH,
        )
        copy.start()
        copy.wait()
        last = r == n_rounds - 1
        dst = out_ref if last else acc[r]
        combine_rows(dst, src, bits[r] * half, recv[r], bits[r] == 1, half, last)
        src = dst


def render_composite(density, bins, table, depth_scale, n_rounds):
    planes, rows, width = density.shape
    lane_rounds = 0
    while (width >> (lane_rounds + 1)) >= LANES and lane_rounds < n_rounds:
        lane_rounds += 1
    n_chunks = rows // ROW_BLOCK
    shapes = []
    for r in range(n_rounds):
        half = width >> (r + 1)
        shapes.append((4, rows, half) if r < lane_rounds else (4, half, rows))
    scratch = [
        pltpu.VMEM((4, rows, width), jnp.float32),
        pltpu.VMEM((6, rows, width), jnp.float32),
        pltpu.VMEM((rows, width), jnp.float32),
        pltpu.VMEM((rows, width), jnp.float32),
        pltpu.VMEM((planes, 8, width), jnp.float32),
        pltpu.VMEM((planes, 8, width), jnp.float32),
        pltpu.SemaphoreType.DMA((4,)),
        pltpu.SemaphoreType.DMA((4,)),
    ]
    scratch += [pltpu.VMEM(s, jnp.float32) for s in shapes]
    scratch += [pltpu.VMEM(s, jnp.float32) for s in shapes[:-1]]
    scratch += [pltpu.VMEM((4, width >> lane_rounds, rows), jnp.float32)]
    n_sems = lane_rounds * n_chunks + n_rounds - lane_rounds
    scratch += [pltpu.SemaphoreType.DMA((n_sems,)), pltpu.SemaphoreType.DMA((n_sems,))]
    vmem = pl.BlockSpec(memory_space=pltpu.VMEM)
    out = pl.pallas_call(
        functools.partial(fused_kernel, depth_scale, n_rounds, lane_rounds, n_chunks),
        out_shape=jax.ShapeDtypeStruct(shapes[-1], jnp.float32),
        in_specs=[vmem] * 3,
        out_specs=vmem,
        scratch_shapes=scratch,
        compiler_params=pltpu.CompilerParams(
            collective_id=0, has_side_effects=True, vmem_limit_bytes=48 * 1024 * 1024),
    )(table, density, bins)
    return jnp.transpose(out, (0, 2, 1))


def per_device(density, bins, colors, extinction):
    depth_cells = density.shape[0]
    slab_count = lax.axis_size("depth")
    depth_scale = 0.6 / (depth_cells * slab_count)
    lookup = jnp.concatenate([colors, extinction[None, :]], 0).astype(jnp.float32)
    table = jnp.concatenate([lookup, jnp.zeros((4, lookup.shape[1]), jnp.float32)], 0)
    return render_composite(density, bins, table, depth_scale, slab_count.bit_length() - 1)


def solution(mesh):
    return jax.shard_map(
        per_device,
        mesh=mesh,
        in_specs=(P("depth", "tile", None), P("depth", "tile", None), P(), P()),
        out_specs=P(None, "tile", "depth"),
        check_vma=False,
    )
```

```python
import functools

import jax
import jax.numpy as jnp
from jax import lax
from jax.experimental import pallas as pl
from jax.experimental.pallas import tpu as pltpu
from jax.sharding import PartitionSpec as P

ROW_BLOCK = 16
LANES = 128
LOOK_ROWS = 128
SHADE_UNROLL = 2


def make_look(tables):
    def look(idx):
        low = idx & (LANES - 1)
        high = idx >= LANES
        vals = []
        for lo_t, hi_t in tables:
            lo_v = jnp.take_along_axis(lo_t, low, axis=1, mode="promise_in_bounds")
            hi_v = jnp.take_along_axis(hi_t, low, axis=1, mode="promise_in_bounds")
            vals.append(jnp.where(high, hi_v, lo_v))
        return vals

    return look


def lookup_rows(depth_scale, look, b_ref, stash_ref, img_ref):
    rows = b_ref.shape[1]
    groups = b_ref.shape[2] // LANES

    per_step = min(LOOK_ROWS, rows) // 8

    def body(i, carry):
        g = i % groups
        k0 = (i // groups) * per_step
        col = pl.ds(pl.multiple_of(g * LANES, LANES), LANES)
        for kk in range(per_step):
            r_sl = pl.ds(pl.multiple_of((k0 + kk) * 8, 8), 8)
            e0 = look(b_ref[0, r_sl, col])
            e1 = look(b_ref[1, r_sl, col])
            o0 = e0[3] * depth_scale
            o1 = e1[3] * depth_scale
            a0 = 1.0 - jnp.exp(-o0)
            a1 = 1.0 - jnp.exp(-o1)
            t0 = jnp.exp(-o0)
            for ch in range(3):
                stash_ref[ch, r_sl, col] = e0[ch] * a0
                stash_ref[3 + ch, r_sl, col] = t0 * (e1[ch] * a1)
            img_ref[3, r_sl, col] = jnp.exp(-(o0 + o1))
        return carry

    lax.fori_loop(0, (rows // 8 // per_step) * groups, body, 0)


def shade_rows(c, n_chunks, d_ref, htop_ref, hbot_ref, xp_ref, xn_ref, has_top, has_bot,
               has_prev, has_next, stash_ref, img_ref):
    row_block = d_ref.shape[1] // n_chunks
    chunks = row_block // 8
    groups = d_ref.shape[2] // LANES
    base = c * row_block
    sub = lax.broadcasted_iota(jnp.int32, (8, LANES), 0)
    lane = lax.broadcasted_iota(jnp.int32, (8, LANES), 1)

    def group_body(g, carry):
        col = pl.ds(pl.multiple_of(g * LANES, LANES), LANES)
        col_l = pl.ds(pl.multiple_of(jnp.maximum(g - 1, 0) * LANES, LANES), LANES)
        col_r = pl.ds(pl.multiple_of(jnp.minimum(g + 1, groups - 1) * LANES, LANES), LANES)
        has_l = g > 0
        has_r = g < groups - 1
        centers = [[d_ref[p, pl.ds(base + k * 8, 8), col] for k in range(chunks)] for p in range(2)]
        for k in range(chunks):
            rows = pl.ds(base + k * 8, 8)
            shades = []
            for p in range(2):
                c_v = centers[p][k]
                if k > 0:
                    up_src = centers[p][k - 1]
                elif c == 0:
                    up_src = jnp.where(has_top, htop_ref[p, :, col], 0.0)
                else:
                    up_src = d_ref[p, pl.ds(base - 8, 8), col]
                if k < chunks - 1:
                    dn_src = centers[p][k + 1]
                elif c == n_chunks - 1:
                    dn_src = jnp.where(has_bot, hbot_ref[p, :, col], 0.0)
                else:
                    dn_src = d_ref[p, pl.ds(base + row_block, 8), col]
                up = jnp.where(sub == 0, pltpu.roll(up_src, 1, 0), pltpu.roll(c_v, 1, 0))
                dn = jnp.where(sub == 7, pltpu.roll(dn_src, 7, 0), pltpu.roll(c_v, 7, 0))
                grad_y = (dn - up) * 0.5
                left_src = jnp.where(has_l, d_ref[p, rows, col_l], 0.0)
                right_src = jnp.where(has_r, d_ref[p, rows, col_r], 0.0)
                lf = jnp.where(lane == 0, pltpu.roll(left_src, 1, 1), pltpu.roll(c_v, 1, 1))
                rt = jnp.where(lane == LANES - 1, pltpu.roll(right_src, LANES - 1, 1),
                               pltpu.roll(c_v, LANES - 1, 1))
                grad_z = (rt - lf) * 0.5
                if p == 0:
                    grad_x = (centers[1][k] - jnp.where(has_prev, xp_ref[rows, col], 0.0)) * 0.5
                else:
                    grad_x = (jnp.where(has_next, xn_ref[rows, col], 0.0) - centers[0][k]) * 0.5
                lit = jnp.abs(0.48 * grad_x + 0.6 * grad_y + 0.64 * grad_z)
                shades.append(0.3 + 0.7 * lit / jnp.sqrt(
                    grad_x * grad_x + grad_y * grad_y + grad_z * grad_z + 1.0))
            for ch in range(3):
                img_ref[ch, rows, col] = (stash_ref[ch, rows, col] * shades[0]
                                          + stash_ref[3 + ch, rows, col] * shades[1])
        return carry

    lax.fori_loop(0, groups, group_body, 0, unroll=SHADE_UNROLL)


def combine_lanes(dst_ref, src_ref, keep_off, rcv_ref, behind, row0, n_rows, half):
    lanes = min(half, LANES)
    groups = half // lanes

    def body(i, carry):
        r_sl = pl.ds(pl.multiple_of(row0 + i * 8, 8), 8)
        for j in range(groups):
            k_sl = pl.ds(pl.multiple_of(keep_off + j * lanes, lanes), lanes)
            d_sl = pl.ds(j * lanes, lanes)
            kept = [src_ref[ch, r_sl, k_sl] for ch in range(4)]
            rcv = [rcv_ref[ch, r_sl, d_sl] for ch in range(4)]
            front = [jnp.where(behind, q, k) for k, q in zip(kept, rcv)]
            back = [jnp.where(behind, k, q) for k, q in zip(kept, rcv)]
            for ch in range(3):
                dst_ref[ch, r_sl, d_sl] = front[ch] + front[3] * back[ch]
            dst_ref[3, r_sl, d_sl] = front[3] * back[3]
        return carry

    lax.fori_loop(0, n_rows // 8, body, 0)


def combine_rows(dst_ref, src_ref, keep_off, rcv_ref, behind, half, finish):
    def body(i, carry):
        r_k = pl.ds(pl.multiple_of(keep_off + i * 8, 8), 8)
        r_d = pl.ds(pl.multiple_of(i * 8, 8), 8)
        kept = [src_ref[ch, r_k, :] for ch in range(4)]
        rcv = [rcv_ref[ch, r_d, :] for ch in range(4)]
        front = [jnp.where(behind, q, k) for k, q in zip(kept, rcv)]
        back = [jnp.where(behind, k, q) for k, q in zip(kept, rcv)]
        for ch in range(3):
            dst_ref[ch, r_d, :] = front[ch] + front[3] * back[ch]
        trans = front[3] * back[3]
        dst_ref[3, r_d, :] = (1.0 - trans) if finish else trans
        return carry

    lax.fori_loop(0, half // 8, body, 0)


def fused_kernel(depth_scale, n_rounds, lane_rounds, n_chunks, table_ref, d_ref, b_ref, out_ref,
                 img_ref, stash_ref, xp_ref, xn_ref, htop_ref, hbot_ref, halo_send, halo_recv, *scratch):
    recv = scratch[:n_rounds]
    acc = scratch[n_rounds:2 * n_rounds - 1]
    flip_ref = scratch[2 * n_rounds - 1]
    send_sems, recv_sems = scratch[2 * n_rounds:]
    me = lax.axis_index("depth")
    tile = lax.axis_index("tile")
    n_slabs = lax.axis_size("depth")
    n_tiles = lax.axis_size("tile")
    bits = [(me // (1 << r)) % 2 for r in range(n_rounds)]
    partners = [me + (1 - 2 * bits[r]) * (1 << r) for r in range(n_rounds)]
    rows = d_ref.shape[1]
    width = d_ref.shape[2]
    row_block = rows // n_chunks
    halves = [width >> (r + 1) for r in range(n_rounds)]
    srcs = [img_ref] + list(acc)
    mesh_id = pl.DeviceIdType.MESH
    has_prev = me > 0
    has_next = me < n_slabs - 1
    has_top = tile > 0
    has_bot = tile < n_tiles - 1
    odd = bits[0] == 1
    extra_nb = jnp.where(odd, has_next, has_prev)
    extra_id = jnp.where(odd, me + 1, me - 1)

    barrier = pltpu.get_barrier_semaphore()
    for r in range(n_rounds):
        pl.semaphore_signal(barrier, inc=1, device_id=(partners[r], tile), device_id_type=mesh_id)

    @pl.when(extra_nb)
    def _():
        pl.semaphore_signal(barrier, inc=1, device_id=(extra_id, tile), device_id_type=mesh_id)

    @pl.when(has_top)
    def _():
        pl.semaphore_signal(barrier, inc=1, device_id=(me, tile - 1), device_id_type=mesh_id)

    @pl.when(has_bot)
    def _():
        pl.semaphore_signal(barrier, inc=1, device_id=(me, tile + 1), device_id_type=mesh_id)

    n_greet = (n_rounds + extra_nb.astype(jnp.int32) + has_top.astype(jnp.int32)
               + has_bot.astype(jnp.int32))
    pl.semaphore_wait(barrier, n_greet)

    halo_copies = [
        (has_next, has_prev, pltpu.make_async_remote_copy(
            src_ref=d_ref.at[1], dst_ref=xp_ref, send_sem=halo_send.at[0],
            recv_sem=halo_recv.at[0], device_id=(me + 1, tile), device_id_type=mesh_id)),
        (has_prev, has_next, pltpu.make_async_remote_copy(
            src_ref=d_ref.at[0], dst_ref=xn_ref, send_sem=halo_send.at[1],
            recv_sem=halo_recv.at[1], device_id=(me - 1, tile), device_id_type=mesh_id)),
        (has_bot, has_top, pltpu.make_async_remote_copy(
            src_ref=d_ref.at[:, pl.ds(rows - 8, 8), :], dst_ref=htop_ref, send_sem=halo_send.at[2],
            recv_sem=halo_recv.at[2], device_id=(me, tile + 1), device_id_type=mesh_id)),
        (has_top, has_bot, pltpu.make_async_remote_copy(
            src_ref=d_ref.at[:, pl.ds(0, 8), :], dst_ref=hbot_ref, send_sem=halo_send.at[3],
            recv_sem=halo_recv.at[3], device_id=(me, tile - 1), device_id_type=mesh_id)),
    ]
    for send_if, _, copy in halo_copies:
        pl.when(send_if)(copy.start)

    tables = [
        (jnp.broadcast_to(table_ref[ch:ch + 1, 0:LANES], (8, LANES)),
         jnp.broadcast_to(table_ref[ch:ch + 1, LANES:2 * LANES], (8, LANES)))
        for ch in range(4)
    ]
    lookup_rows(depth_scale, make_look(tables), b_ref, stash_ref, img_ref)
    for send_if, recv_if, copy in halo_copies:
        pl.when(send_if)(copy.wait_send)
        pl.when(recv_if)(copy.wait_recv)
    copies = {}

    def start_lane(r, c):
        row_sl = pl.ds(c * row_block, row_block)
        send_off = pl.multiple_of((1 - bits[r]) * halves[r], LANES)
        copy = pltpu.make_async_remote_copy(
            src_ref=srcs[r].at[:, row_sl, pl.ds(send_off, halves[r])],
            dst_ref=recv[r].at[:, row_sl, :],
            send_sem=send_sems.at[r * n_chunks + c],
            recv_sem=recv_sems.at[r * n_chunks + c],
            device_id=(partners[r], tile),
            device_id_type=pl.DeviceIdType.MESH,
        )
        copy.start()
        copies[(r, c)] = copy

    def finish_lane(r, c):
        copies[(r, c)].wait()
        combine_lanes(acc[r], srcs[r], bits[r] * halves[r], recv[r], bits[r] == 1,
                      c * row_block, row_block, halves[r])
        if r + 1 < lane_rounds:
            start_lane(r + 1, c)

    for c in range(n_chunks):
        shade_rows(c, n_chunks, d_ref, htop_ref, hbot_ref, xp_ref, xn_ref, has_top, has_bot,
                   has_prev, has_next, stash_ref, img_ref)
        start_lane(0, c)
        if c >= 1:
            finish_lane(0, c - 1)
    finish_lane(0, n_chunks - 1)
    for r in range(1, lane_rounds):
        for c in range(n_chunks):
            finish_lane(r, c)

    src = acc[lane_rounds - 1]
    for ch in range(4):
        flip_ref[ch] = src[ch].T
    src = flip_ref
    sem_base = lane_rounds * n_chunks
    for r in range(lane_rounds, n_rounds):
        half = halves[r]
        send_off = pl.multiple_of((1 - bits[r]) * half, 8)
        copy = pltpu.make_async_remote_copy(
            src_ref=src.at[:, pl.ds(send_off, half), :],
            dst_ref=recv[r],
            send_sem=send_sems.at[sem_base + r - lane_rounds],
            recv_sem=recv_sems.at[sem_base + r - lane_rounds],
            device_id=(partners[r], tile),
            device_id_type=pl.DeviceIdType.MESH,
        )
        copy.start()
        copy.wait()
        last = r == n_rounds - 1
        dst = out_ref if last else acc[r]
        combine_rows(dst, src, bits[r] * half, recv[r], bits[r] == 1, half, last)
        src = dst


def render_composite(density, bins, table, depth_scale, n_rounds):
    planes, rows, width = density.shape
    lane_rounds = 0
    while (width >> (lane_rounds + 1)) >= LANES and lane_rounds < n_rounds:
        lane_rounds += 1
    n_chunks = rows // ROW_BLOCK
    shapes = []
    for r in range(n_rounds):
        half = width >> (r + 1)
        shapes.append((4, rows, half) if r < lane_rounds else (4, half, rows))
    scratch = [
        pltpu.VMEM((4, rows, width), jnp.float32),
        pltpu.VMEM((6, rows, width), jnp.float32),
        pltpu.VMEM((rows, width), jnp.float32),
        pltpu.VMEM((rows, width), jnp.float32),
        pltpu.VMEM((planes, 8, width), jnp.float32),
        pltpu.VMEM((planes, 8, width), jnp.float32),
        pltpu.SemaphoreType.DMA((4,)),
        pltpu.SemaphoreType.DMA((4,)),
    ]
    scratch += [pltpu.VMEM(s, jnp.float32) for s in shapes]
    scratch += [pltpu.VMEM(s, jnp.float32) for s in shapes[:-1]]
    scratch += [pltpu.VMEM((4, width >> lane_rounds, rows), jnp.float32)]
    n_sems = lane_rounds * n_chunks + n_rounds - lane_rounds
    scratch += [pltpu.SemaphoreType.DMA((n_sems,)), pltpu.SemaphoreType.DMA((n_sems,))]
    vmem = pl.BlockSpec(memory_space=pltpu.VMEM)
    out = pl.pallas_call(
        functools.partial(fused_kernel, depth_scale, n_rounds, lane_rounds, n_chunks),
        out_shape=jax.ShapeDtypeStruct(shapes[-1], jnp.float32),
        in_specs=[vmem] * 3,
        out_specs=vmem,
        scratch_shapes=scratch,
        compiler_params=pltpu.CompilerParams(
            collective_id=0, has_side_effects=True, vmem_limit_bytes=48 * 1024 * 1024),
    )(table, density, bins)
    return jnp.transpose(out, (0, 2, 1))


def per_device(density, bins, colors, extinction):
    depth_cells = density.shape[0]
    slab_count = lax.axis_size("depth")
    depth_scale = 0.6 / (depth_cells * slab_count)
    lookup = jnp.concatenate([colors, extinction[None, :]], 0).astype(jnp.float32)
    table = jnp.concatenate([lookup, jnp.zeros((4, lookup.shape[1]), jnp.float32)], 0)
    return render_composite(density, bins, table, depth_scale, slab_count.bit_length() - 1)


def solution(mesh):
    return jax.shard_map(
        per_device,
        mesh=mesh,
        in_specs=(P("depth", "tile", None), P("depth", "tile", None), P(), P()),
        out_specs=P(None, "tile", "depth"),
        check_vma=False,
    )
```

```python
import functools

import jax
import jax.numpy as jnp
from jax import lax
from jax.experimental import pallas as pl
from jax.experimental.pallas import tpu as pltpu
from jax.sharding import PartitionSpec as P

ROW_BLOCK = 16
LANES = 128
LOOK_UNROLL = 4
SHADE_UNROLL = 2


def make_look(tables):
    def look(idx):
        low = idx & (LANES - 1)
        high = idx >= LANES
        vals = []
        for lo_t, hi_t in tables:
            lo_v = jnp.take_along_axis(lo_t, low, axis=1, mode="promise_in_bounds")
            hi_v = jnp.take_along_axis(hi_t, low, axis=1, mode="promise_in_bounds")
            vals.append(jnp.where(high, hi_v, lo_v))
        return vals

    return look


def lookup_rows(depth_scale, look, b_ref, stash_ref, img_ref, row0, n_rows):
    groups = b_ref.shape[2] // LANES
    per_step = n_rows // 8

    def body(g, carry):
        col = pl.ds(pl.multiple_of(g * LANES, LANES), LANES)
        for kk in range(per_step):
            r_sl = pl.ds(row0 + kk * 8, 8)
            e0 = look(b_ref[0, r_sl, col])
            e1 = look(b_ref[1, r_sl, col])
            o0 = e0[3] * depth_scale
            o1 = e1[3] * depth_scale
            a0 = 1.0 - jnp.exp(-o0)
            a1 = 1.0 - jnp.exp(-o1)
            t0 = jnp.exp(-o0)
            for ch in range(3):
                stash_ref[ch, r_sl, col] = e0[ch] * a0
                stash_ref[3 + ch, r_sl, col] = t0 * (e1[ch] * a1)
            img_ref[3, r_sl, col] = jnp.exp(-(o0 + o1))
        return carry

    lax.fori_loop(0, groups, body, 0, unroll=LOOK_UNROLL)


def shade_rows(c, n_chunks, d_ref, htop_ref, hbot_ref, xp_ref, xn_ref, has_top, has_bot,
               has_prev, has_next, stash_ref, img_ref):
    row_block = d_ref.shape[1] // n_chunks
    chunks = row_block // 8
    groups = d_ref.shape[2] // LANES
    base = c * row_block
    sub = lax.broadcasted_iota(jnp.int32, (8, LANES), 0)
    lane = lax.broadcasted_iota(jnp.int32, (8, LANES), 1)

    def group_body(g, carry):
        col = pl.ds(pl.multiple_of(g * LANES, LANES), LANES)
        col_l = pl.ds(pl.multiple_of(jnp.maximum(g - 1, 0) * LANES, LANES), LANES)
        col_r = pl.ds(pl.multiple_of(jnp.minimum(g + 1, groups - 1) * LANES, LANES), LANES)
        has_l = g > 0
        has_r = g < groups - 1
        centers = [[d_ref[p, pl.ds(base + k * 8, 8), col] for k in range(chunks)] for p in range(2)]
        for k in range(chunks):
            rows = pl.ds(base + k * 8, 8)
            shades = []
            for p in range(2):
                c_v = centers[p][k]
                if k > 0:
                    up_src = centers[p][k - 1]
                elif c == 0:
                    up_src = jnp.where(has_top, htop_ref[p, :, col], 0.0)
                else:
                    up_src = d_ref[p, pl.ds(base - 8, 8), col]
                if k < chunks - 1:
                    dn_src = centers[p][k + 1]
                elif c == n_chunks - 1:
                    dn_src = jnp.where(has_bot, hbot_ref[p, :, col], 0.0)
                else:
                    dn_src = d_ref[p, pl.ds(base + row_block, 8), col]
                up = jnp.where(sub == 0, pltpu.roll(up_src, 1, 0), pltpu.roll(c_v, 1, 0))
                dn = jnp.where(sub == 7, pltpu.roll(dn_src, 7, 0), pltpu.roll(c_v, 7, 0))
                grad_y = (dn - up) * 0.5
                left_src = jnp.where(has_l, d_ref[p, rows, col_l], 0.0)
                right_src = jnp.where(has_r, d_ref[p, rows, col_r], 0.0)
                lf = jnp.where(lane == 0, pltpu.roll(left_src, 1, 1), pltpu.roll(c_v, 1, 1))
                rt = jnp.where(lane == LANES - 1, pltpu.roll(right_src, LANES - 1, 1),
                               pltpu.roll(c_v, LANES - 1, 1))
                grad_z = (rt - lf) * 0.5
                if p == 0:
                    grad_x = (centers[1][k] - jnp.where(has_prev, xp_ref[rows, col], 0.0)) * 0.5
                else:
                    grad_x = (jnp.where(has_next, xn_ref[rows, col], 0.0) - centers[0][k]) * 0.5
                lit = jnp.abs(0.48 * grad_x + 0.6 * grad_y + 0.64 * grad_z)
                shades.append(0.3 + 0.7 * lit / jnp.sqrt(
                    grad_x * grad_x + grad_y * grad_y + grad_z * grad_z + 1.0))
            for ch in range(3):
                img_ref[ch, rows, col] = (stash_ref[ch, rows, col] * shades[0]
                                          + stash_ref[3 + ch, rows, col] * shades[1])
        return carry

    lax.fori_loop(0, groups, group_body, 0, unroll=SHADE_UNROLL)


def combine_lanes(dst_ref, src_ref, keep_off, rcv_ref, behind, row0, n_rows, half):
    lanes = min(half, LANES)
    groups = half // lanes

    def body(i, carry):
        r_sl = pl.ds(pl.multiple_of(row0 + i * 8, 8), 8)
        for j in range(groups):
            k_sl = pl.ds(pl.multiple_of(keep_off + j * lanes, lanes), lanes)
            d_sl = pl.ds(j * lanes, lanes)
            kept = [src_ref[ch, r_sl, k_sl] for ch in range(4)]
            rcv = [rcv_ref[ch, r_sl, d_sl] for ch in range(4)]
            front = [jnp.where(behind, q, k) for k, q in zip(kept, rcv)]
            back = [jnp.where(behind, k, q) for k, q in zip(kept, rcv)]
            for ch in range(3):
                dst_ref[ch, r_sl, d_sl] = front[ch] + front[3] * back[ch]
            dst_ref[3, r_sl, d_sl] = front[3] * back[3]
        return carry

    lax.fori_loop(0, n_rows // 8, body, 0)


def combine_rows(dst_ref, src_ref, keep_off, rcv_ref, behind, half, finish):
    def body(i, carry):
        r_k = pl.ds(pl.multiple_of(keep_off + i * 8, 8), 8)
        r_d = pl.ds(pl.multiple_of(i * 8, 8), 8)
        kept = [src_ref[ch, r_k, :] for ch in range(4)]
        rcv = [rcv_ref[ch, r_d, :] for ch in range(4)]
        front = [jnp.where(behind, q, k) for k, q in zip(kept, rcv)]
        back = [jnp.where(behind, k, q) for k, q in zip(kept, rcv)]
        for ch in range(3):
            dst_ref[ch, r_d, :] = front[ch] + front[3] * back[ch]
        trans = front[3] * back[3]
        dst_ref[3, r_d, :] = (1.0 - trans) if finish else trans
        return carry

    lax.fori_loop(0, half // 8, body, 0)


def fused_kernel(depth_scale, n_rounds, lane_rounds, n_chunks, table_ref, d_ref, b_ref, out_ref,
                 img_ref, stash_ref, xp_ref, xn_ref, htop_ref, hbot_ref, halo_send, halo_recv, *scratch):
    recv = scratch[:n_rounds]
    acc = scratch[n_rounds:2 * n_rounds - 1]
    flip_ref = scratch[2 * n_rounds - 1]
    send_sems, recv_sems = scratch[2 * n_rounds:]
    me = lax.axis_index("depth")
    tile = lax.axis_index("tile")
    n_slabs = lax.axis_size("depth")
    n_tiles = lax.axis_size("tile")
    bits = [(me // (1 << r)) % 2 for r in range(n_rounds)]
    partners = [me + (1 - 2 * bits[r]) * (1 << r) for r in range(n_rounds)]
    rows = d_ref.shape[1]
    width = d_ref.shape[2]
    row_block = rows // n_chunks
    halves = [width >> (r + 1) for r in range(n_rounds)]
    srcs = [img_ref] + list(acc)
    mesh_id = pl.DeviceIdType.MESH
    has_prev = me > 0
    has_next = me < n_slabs - 1
    has_top = tile > 0
    has_bot = tile < n_tiles - 1
    odd = bits[0] == 1
    extra_nb = jnp.where(odd, has_next, has_prev)
    extra_id = jnp.where(odd, me + 1, me - 1)

    barrier = pltpu.get_barrier_semaphore()
    for r in range(n_rounds):
        pl.semaphore_signal(barrier, inc=1, device_id=(partners[r], tile), device_id_type=mesh_id)

    @pl.when(extra_nb)
    def _():
        pl.semaphore_signal(barrier, inc=1, device_id=(extra_id, tile), device_id_type=mesh_id)

    @pl.when(has_top)
    def _():
        pl.semaphore_signal(barrier, inc=1, device_id=(me, tile - 1), device_id_type=mesh_id)

    @pl.when(has_bot)
    def _():
        pl.semaphore_signal(barrier, inc=1, device_id=(me, tile + 1), device_id_type=mesh_id)

    n_greet = (n_rounds + extra_nb.astype(jnp.int32) + has_top.astype(jnp.int32)
               + has_bot.astype(jnp.int32))
    pl.semaphore_wait(barrier, n_greet)

    def halo(send_if, recv_if, src_ref, dst_ref, idx, dev):
        return (send_if, recv_if, pltpu.make_async_remote_copy(
            src_ref=src_ref, dst_ref=dst_ref, send_sem=halo_send.at[idx],
            recv_sem=halo_recv.at[idx], device_id=dev, device_id_type=mesh_id))

    edge_copies = [
        halo(has_bot, has_top, d_ref.at[:, pl.ds(rows - 8, 8), :], htop_ref, 0, (me, tile + 1)),
        halo(has_top, has_bot, d_ref.at[:, pl.ds(0, 8), :], hbot_ref, 1, (me, tile - 1)),
    ]
    plane_copies = []
    for c in range(n_chunks):
        row_sl = pl.ds(c * row_block, row_block)
        plane_copies.append((
            halo(has_next, has_prev, d_ref.at[1, row_sl, :], xp_ref.at[row_sl, :], 2 + 2 * c,
                 (me + 1, tile)),
            halo(has_prev, has_next, d_ref.at[0, row_sl, :], xn_ref.at[row_sl, :], 3 + 2 * c,
                 (me - 1, tile)),
        ))
    all_halos = edge_copies + [h for pair in plane_copies for h in pair]
    for send_if, _, copy in all_halos:
        pl.when(send_if)(copy.start)

    tables = [
        (jnp.broadcast_to(table_ref[ch:ch + 1, 0:LANES], (8, LANES)),
         jnp.broadcast_to(table_ref[ch:ch + 1, LANES:2 * LANES], (8, LANES)))
        for ch in range(4)
    ]
    look = make_look(tables)
    copies = {}

    def start_lane(r, c):
        row_sl = pl.ds(c * row_block, row_block)
        send_off = pl.multiple_of((1 - bits[r]) * halves[r], LANES)
        copy = pltpu.make_async_remote_copy(
            src_ref=srcs[r].at[:, row_sl, pl.ds(send_off, halves[r])],
            dst_ref=recv[r].at[:, row_sl, :],
            send_sem=send_sems.at[r * n_chunks + c],
            recv_sem=recv_sems.at[r * n_chunks + c],
            device_id=(partners[r], tile),
            device_id_type=pl.DeviceIdType.MESH,
        )
        copy.start()
        copies[(r, c)] = copy

    def finish_lane(r, c):
        copies[(r, c)].wait()
        combine_lanes(acc[r], srcs[r], bits[r] * halves[r], recv[r], bits[r] == 1,
                      c * row_block, row_block, halves[r])
        if r + 1 < lane_rounds:
            start_lane(r + 1, c)

    for c in range(n_chunks):
        lookup_rows(depth_scale, look, b_ref, stash_ref, img_ref, c * row_block, row_block)
        waits = list(plane_copies[c])
        if c == 0:
            waits.append(edge_copies[0])
        if c == n_chunks - 1:
            waits.append(edge_copies[1])
        for _, recv_if, copy in waits:
            pl.when(recv_if)(copy.wait_recv)
        shade_rows(c, n_chunks, d_ref, htop_ref, hbot_ref, xp_ref, xn_ref, has_top, has_bot,
                   has_prev, has_next, stash_ref, img_ref)
        start_lane(0, c)
        if c >= 1:
            finish_lane(0, c - 1)
    finish_lane(0, n_chunks - 1)
    for r in range(1, lane_rounds):
        for c in range(n_chunks):
            finish_lane(r, c)
    for send_if, _, copy in all_halos:
        pl.when(send_if)(copy.wait_send)

    src = acc[lane_rounds - 1]
    for ch in range(4):
        flip_ref[ch] = src[ch].T
    src = flip_ref
    sem_base = lane_rounds * n_chunks
    for r in range(lane_rounds, n_rounds):
        half = halves[r]
        send_off = pl.multiple_of((1 - bits[r]) * half, 8)
        copy = pltpu.make_async_remote_copy(
            src_ref=src.at[:, pl.ds(send_off, half), :],
            dst_ref=recv[r],
            send_sem=send_sems.at[sem_base + r - lane_rounds],
            recv_sem=recv_sems.at[sem_base + r - lane_rounds],
            device_id=(partners[r], tile),
            device_id_type=pl.DeviceIdType.MESH,
        )
        copy.start()
        copy.wait()
        last = r == n_rounds - 1
        dst = out_ref if last else acc[r]
        combine_rows(dst, src, bits[r] * half, recv[r], bits[r] == 1, half, last)
        src = dst


def render_composite(density, bins, table, depth_scale, n_rounds):
    planes, rows, width = density.shape
    lane_rounds = 0
    while (width >> (lane_rounds + 1)) >= LANES and lane_rounds < n_rounds:
        lane_rounds += 1
    n_chunks = rows // ROW_BLOCK
    shapes = []
    for r in range(n_rounds):
        half = width >> (r + 1)
        shapes.append((4, rows, half) if r < lane_rounds else (4, half, rows))
    scratch = [
        pltpu.VMEM((4, rows, width), jnp.float32),
        pltpu.VMEM((6, rows, width), jnp.float32),
        pltpu.VMEM((rows, width), jnp.float32),
        pltpu.VMEM((rows, width), jnp.float32),
        pltpu.VMEM((planes, 8, width), jnp.float32),
        pltpu.VMEM((planes, 8, width), jnp.float32),
        pltpu.SemaphoreType.DMA((2 + 2 * n_chunks,)),
        pltpu.SemaphoreType.DMA((2 + 2 * n_chunks,)),
    ]
    scratch += [pltpu.VMEM(s, jnp.float32) for s in shapes]
    scratch += [pltpu.VMEM(s, jnp.float32) for s in shapes[:-1]]
    scratch += [pltpu.VMEM((4, width >> lane_rounds, rows), jnp.float32)]
    n_sems = lane_rounds * n_chunks + n_rounds - lane_rounds
    scratch += [pltpu.SemaphoreType.DMA((n_sems,)), pltpu.SemaphoreType.DMA((n_sems,))]
    vmem = pl.BlockSpec(memory_space=pltpu.VMEM)
    out = pl.pallas_call(
        functools.partial(fused_kernel, depth_scale, n_rounds, lane_rounds, n_chunks),
        out_shape=jax.ShapeDtypeStruct(shapes[-1], jnp.float32),
        in_specs=[vmem] * 3,
        out_specs=vmem,
        scratch_shapes=scratch,
        compiler_params=pltpu.CompilerParams(
            collective_id=0, has_side_effects=True, vmem_limit_bytes=48 * 1024 * 1024),
    )(table, density, bins)
    return jnp.transpose(out, (0, 2, 1))


def per_device(density, bins, colors, extinction):
    depth_cells = density.shape[0]
    slab_count = lax.axis_size("depth")
    depth_scale = 0.6 / (depth_cells * slab_count)
    lookup = jnp.concatenate([colors, extinction[None, :]], 0).astype(jnp.float32)
    table = jnp.concatenate([lookup, jnp.zeros((4, lookup.shape[1]), jnp.float32)], 0)
    return render_composite(density, bins, table, depth_scale, slab_count.bit_length() - 1)


def solution(mesh):
    return jax.shard_map(
        per_device,
        mesh=mesh,
        in_specs=(P("depth", "tile", None), P("depth", "tile", None), P(), P()),
        out_specs=P(None, "tile", "depth"),
        check_vma=False,
    )
```

```python
import functools

import jax
import jax.numpy as jnp
from jax import lax
from jax.experimental import pallas as pl
from jax.experimental.pallas import tpu as pltpu
from jax.sharding import PartitionSpec as P

ROW_BLOCK = 16
LANES = 128
LOOK_UNROLL = 4
SHADE_UNROLL = 2


def make_look(tables):
    def look(idx):
        low = idx & (LANES - 1)
        high = idx >= LANES
        vals = []
        for lo_t, hi_t in tables:
            lo_v = jnp.take_along_axis(lo_t, low, axis=1, mode="promise_in_bounds")
            hi_v = jnp.take_along_axis(hi_t, low, axis=1, mode="promise_in_bounds")
            vals.append(jnp.where(high, hi_v, lo_v))
        return vals

    return look


def lookup_rows(depth_scale, look, b_ref, stash_ref, img_ref, row0, n_rows):
    groups = b_ref.shape[2] // LANES
    per_step = n_rows // 8

    def body(g, carry):
        col = pl.ds(pl.multiple_of(g * LANES, LANES), LANES)
        for kk in range(per_step):
            r_sl = pl.ds(row0 + kk * 8, 8)
            e0 = look(b_ref[0, r_sl, col])
            e1 = look(b_ref[1, r_sl, col])
            o0 = e0[3] * depth_scale
            o1 = e1[3] * depth_scale
            a0 = 1.0 - jnp.exp(-o0)
            a1 = 1.0 - jnp.exp(-o1)
            t0 = jnp.exp(-o0)
            for ch in range(3):
                stash_ref[ch, r_sl, col] = e0[ch] * a0
                stash_ref[3 + ch, r_sl, col] = t0 * (e1[ch] * a1)
            img_ref[3, r_sl, col] = jnp.exp(-(o0 + o1))
        return carry

    lax.fori_loop(0, groups, body, 0, unroll=LOOK_UNROLL)


def shade_rows(c, n_chunks, d_ref, htop_ref, hbot_ref, xp_ref, xn_ref, has_top, has_bot,
               has_prev, has_next, stash_ref, img_ref):
    row_block = d_ref.shape[1] // n_chunks
    chunks = row_block // 8
    groups = d_ref.shape[2] // LANES
    base = c * row_block
    sub = lax.broadcasted_iota(jnp.int32, (8, LANES), 0)
    lane = lax.broadcasted_iota(jnp.int32, (8, LANES), 1)

    def group_body(g, carry):
        col = pl.ds(pl.multiple_of(g * LANES, LANES), LANES)
        col_l = pl.ds(pl.multiple_of(jnp.maximum(g - 1, 0) * LANES, LANES), LANES)
        col_r = pl.ds(pl.multiple_of(jnp.minimum(g + 1, groups - 1) * LANES, LANES), LANES)
        has_l = g > 0
        has_r = g < groups - 1
        centers = [[d_ref[p, pl.ds(base + k * 8, 8), col] for k in range(chunks)] for p in range(2)]
        for k in range(chunks):
            rows = pl.ds(base + k * 8, 8)
            shades = []
            for p in range(2):
                c_v = centers[p][k]
                if k > 0:
                    up_src = centers[p][k - 1]
                elif c == 0:
                    up_src = jnp.where(has_top, htop_ref[p, :, col], 0.0)
                else:
                    up_src = d_ref[p, pl.ds(base - 8, 8), col]
                if k < chunks - 1:
                    dn_src = centers[p][k + 1]
                elif c == n_chunks - 1:
                    dn_src = jnp.where(has_bot, hbot_ref[p, :, col], 0.0)
                else:
                    dn_src = d_ref[p, pl.ds(base + row_block, 8), col]
                up = jnp.where(sub == 0, pltpu.roll(up_src, 1, 0), pltpu.roll(c_v, 1, 0))
                dn = jnp.where(sub == 7, pltpu.roll(dn_src, 7, 0), pltpu.roll(c_v, 7, 0))
                grad_y = (dn - up) * 0.5
                left_src = jnp.where(has_l, d_ref[p, rows, col_l], 0.0)
                right_src = jnp.where(has_r, d_ref[p, rows, col_r], 0.0)
                lf = jnp.where(lane == 0, pltpu.roll(left_src, 1, 1), pltpu.roll(c_v, 1, 1))
                rt = jnp.where(lane == LANES - 1, pltpu.roll(right_src, LANES - 1, 1),
                               pltpu.roll(c_v, LANES - 1, 1))
                grad_z = (rt - lf) * 0.5
                if p == 0:
                    grad_x = (centers[1][k] - jnp.where(has_prev, xp_ref[rows, col], 0.0)) * 0.5
                else:
                    grad_x = (jnp.where(has_next, xn_ref[rows, col], 0.0) - centers[0][k]) * 0.5
                lit = jnp.abs(0.48 * grad_x + 0.6 * grad_y + 0.64 * grad_z)
                shades.append(0.3 + 0.7 * lit / jnp.sqrt(
                    grad_x * grad_x + grad_y * grad_y + grad_z * grad_z + 1.0))
            for ch in range(3):
                img_ref[ch, rows, col] = (stash_ref[ch, rows, col] * shades[0]
                                          + stash_ref[3 + ch, rows, col] * shades[1])
        return carry

    lax.fori_loop(0, groups, group_body, 0, unroll=SHADE_UNROLL)


def combine_lanes(dst_ref, src_ref, keep_off, rcv_ref, behind, row0, n_rows, half):
    lanes = min(half, LANES)
    groups = half // lanes

    def body(i, carry):
        r_sl = pl.ds(pl.multiple_of(row0 + i * 8, 8), 8)
        for j in range(groups):
            k_sl = pl.ds(pl.multiple_of(keep_off + j * lanes, lanes), lanes)
            d_sl = pl.ds(j * lanes, lanes)
            kept = [src_ref[ch, r_sl, k_sl] for ch in range(4)]
            rcv = [rcv_ref[ch, r_sl, d_sl] for ch in range(4)]
            front = [jnp.where(behind, q, k) for k, q in zip(kept, rcv)]
            back = [jnp.where(behind, k, q) for k, q in zip(kept, rcv)]
            for ch in range(3):
                dst_ref[ch, r_sl, d_sl] = front[ch] + front[3] * back[ch]
            dst_ref[3, r_sl, d_sl] = front[3] * back[3]
        return carry

    lax.fori_loop(0, n_rows // 8, body, 0)


def combine_rows(dst_ref, src_ref, keep_off, rcv_ref, behind, half, finish):
    def body(i, carry):
        r_k = pl.ds(pl.multiple_of(keep_off + i * 8, 8), 8)
        r_d = pl.ds(pl.multiple_of(i * 8, 8), 8)
        kept = [src_ref[ch, r_k, :] for ch in range(4)]
        rcv = [rcv_ref[ch, r_d, :] for ch in range(4)]
        front = [jnp.where(behind, q, k) for k, q in zip(kept, rcv)]
        back = [jnp.where(behind, k, q) for k, q in zip(kept, rcv)]
        for ch in range(3):
            dst_ref[ch, r_d, :] = front[ch] + front[3] * back[ch]
        trans = front[3] * back[3]
        dst_ref[3, r_d, :] = (1.0 - trans) if finish else trans
        return carry

    lax.fori_loop(0, half // 8, body, 0)


def fused_kernel(depth_scale, n_rounds, lane_rounds, n_chunks, table_ref, d_ref, b_ref, out_ref,
                 img_ref, stash_ref, xp_ref, xn_ref, htop_ref, hbot_ref, halo_send, halo_recv, *scratch):
    recv = scratch[:n_rounds]
    acc = scratch[n_rounds:2 * n_rounds - 1]
    flip_ref = scratch[2 * n_rounds - 1]
    send_sems, recv_sems, parts_ref, tail_send, tail_recv = scratch[2 * n_rounds:]
    me = lax.axis_index("depth")
    tile = lax.axis_index("tile")
    n_slabs = lax.axis_size("depth")
    n_tiles = lax.axis_size("tile")
    bits = [(me // (1 << r)) % 2 for r in range(n_rounds)]
    partners = [me + (1 - 2 * bits[r]) * (1 << r) for r in range(n_rounds)]
    rows = d_ref.shape[1]
    width = d_ref.shape[2]
    row_block = rows // n_chunks
    halves = [width >> (r + 1) for r in range(n_rounds)]
    srcs = [img_ref] + list(acc)
    mesh_id = pl.DeviceIdType.MESH
    has_prev = me > 0
    has_next = me < n_slabs - 1
    has_top = tile > 0
    has_bot = tile < n_tiles - 1
    odd = bits[0] == 1
    extra_nb = jnp.where(odd, has_next, has_prev)
    extra_id = jnp.where(odd, me + 1, me - 1)

    barrier = pltpu.get_barrier_semaphore()
    for r in range(n_rounds):
        pl.semaphore_signal(barrier, inc=1, device_id=(partners[r], tile), device_id_type=mesh_id)

    @pl.when(extra_nb)
    def _():
        pl.semaphore_signal(barrier, inc=1, device_id=(extra_id, tile), device_id_type=mesh_id)

    @pl.when(has_top)
    def _():
        pl.semaphore_signal(barrier, inc=1, device_id=(me, tile - 1), device_id_type=mesh_id)

    @pl.when(has_bot)
    def _():
        pl.semaphore_signal(barrier, inc=1, device_id=(me, tile + 1), device_id_type=mesh_id)

    direct = n_rounds - lane_rounds == 2
    group_step = 1 << lane_rounds
    member = (me // group_step) % 4
    group_base = me - member * group_step
    if direct:
        pl.semaphore_signal(barrier, inc=1, device_id=(group_base + (3 - member) * group_step, tile),
                            device_id_type=mesh_id)
    n_greet = (n_rounds + int(direct) + extra_nb.astype(jnp.int32) + has_top.astype(jnp.int32)
               + has_bot.astype(jnp.int32))
    pl.semaphore_wait(barrier, n_greet)

    def halo(send_if, recv_if, src_ref, dst_ref, idx, dev):
        return (send_if, recv_if, pltpu.make_async_remote_copy(
            src_ref=src_ref, dst_ref=dst_ref, send_sem=halo_send.at[idx],
            recv_sem=halo_recv.at[idx], device_id=dev, device_id_type=mesh_id))

    edge_copies = [
        halo(has_bot, has_top, d_ref.at[:, pl.ds(rows - 8, 8), :], htop_ref, 0, (me, tile + 1)),
        halo(has_top, has_bot, d_ref.at[:, pl.ds(0, 8), :], hbot_ref, 1, (me, tile - 1)),
    ]
    plane_copies = []
    for c in range(n_chunks):
        row_sl = pl.ds(c * row_block, row_block)
        plane_copies.append((
            halo(has_next, has_prev, d_ref.at[1, row_sl, :], xp_ref.at[row_sl, :], 2 + 2 * c,
                 (me + 1, tile)),
            halo(has_prev, has_next, d_ref.at[0, row_sl, :], xn_ref.at[row_sl, :], 3 + 2 * c,
                 (me - 1, tile)),
        ))
    all_halos = edge_copies + [h for pair in plane_copies for h in pair]
    for send_if, _, copy in all_halos:
        pl.when(send_if)(copy.start)

    tables = [
        (jnp.broadcast_to(table_ref[ch:ch + 1, 0:LANES], (8, LANES)),
         jnp.broadcast_to(table_ref[ch:ch + 1, LANES:2 * LANES], (8, LANES)))
        for ch in range(4)
    ]
    look = make_look(tables)
    copies = {}

    def start_lane(r, c):
        row_sl = pl.ds(c * row_block, row_block)
        send_off = pl.multiple_of((1 - bits[r]) * halves[r], LANES)
        copy = pltpu.make_async_remote_copy(
            src_ref=srcs[r].at[:, row_sl, pl.ds(send_off, halves[r])],
            dst_ref=recv[r].at[:, row_sl, :],
            send_sem=send_sems.at[r * n_chunks + c],
            recv_sem=recv_sems.at[r * n_chunks + c],
            device_id=(partners[r], tile),
            device_id_type=pl.DeviceIdType.MESH,
        )
        copy.start()
        copies[(r, c)] = copy

    def finish_lane(r, c):
        copies[(r, c)].wait()
        combine_lanes(acc[r], srcs[r], bits[r] * halves[r], recv[r], bits[r] == 1,
                      c * row_block, row_block, halves[r])
        if r + 1 < lane_rounds:
            start_lane(r + 1, c)

    for c in range(n_chunks):
        lookup_rows(depth_scale, look, b_ref, stash_ref, img_ref, c * row_block, row_block)
        waits = list(plane_copies[c])
        if c == 0:
            waits.append(edge_copies[0])
        if c == n_chunks - 1:
            waits.append(edge_copies[1])
        for _, recv_if, copy in waits:
            pl.when(recv_if)(copy.wait_recv)
        shade_rows(c, n_chunks, d_ref, htop_ref, hbot_ref, xp_ref, xn_ref, has_top, has_bot,
                   has_prev, has_next, stash_ref, img_ref)
        start_lane(0, c)
        if c >= 1:
            finish_lane(0, c - 1)
    finish_lane(0, n_chunks - 1)
    for r in range(1, lane_rounds):
        for c in range(n_chunks):
            finish_lane(r, c)
    for send_if, _, copy in all_halos:
        pl.when(send_if)(copy.wait_send)

    src = acc[lane_rounds - 1]
    for ch in range(4):
        flip_ref[ch] = src[ch].T
    src = flip_ref
    if direct:
        quarter = halves[-1]

        def owned(j):
            return (2 * (j % 2) + j // 2) * quarter

        sends = []
        for k in range(1, 4):
            dst_j = (member + k) % 4
            copy = pltpu.make_async_remote_copy(
                src_ref=flip_ref.at[:, pl.ds(pl.multiple_of(owned(dst_j), 8), quarter), :],
                dst_ref=parts_ref.at[member],
                send_sem=tail_send.at[k - 1],
                recv_sem=tail_recv.at[member],
                device_id=(group_base + dst_j * group_step, tile),
                device_id_type=mesh_id,
            )
            copy.start()
            sends.append(copy)
        parts_ref[member] = flip_ref[:, pl.ds(pl.multiple_of(owned(member), 8), quarter), :]
        for k in range(1, 4):
            src_j = (member + 4 - k) % 4
            pltpu.make_async_remote_copy(
                src_ref=flip_ref.at[:, pl.ds(0, quarter), :],
                dst_ref=parts_ref.at[src_j],
                send_sem=tail_send.at[k - 1],
                recv_sem=tail_recv.at[src_j],
                device_id=(group_base + src_j * group_step, tile),
                device_id_type=mesh_id,
            ).wait_recv()
        for copy in sends:
            copy.wait_send()
        front = [parts_ref[0, ch] for ch in range(4)]
        for j in range(1, 4):
            back = [parts_ref[j, ch] for ch in range(4)]
            front = [front[ch] + front[3] * back[ch] for ch in range(3)] + [front[3] * back[3]]
        for ch in range(3):
            out_ref[ch] = front[ch]
        out_ref[3] = 1.0 - front[3]
        return

    sem_base = lane_rounds * n_chunks
    for r in range(lane_rounds, n_rounds):
        half = halves[r]
        send_off = pl.multiple_of((1 - bits[r]) * half, 8)
        copy = pltpu.make_async_remote_copy(
            src_ref=src.at[:, pl.ds(send_off, half), :],
            dst_ref=recv[r],
            send_sem=send_sems.at[sem_base + r - lane_rounds],
            recv_sem=recv_sems.at[sem_base + r - lane_rounds],
            device_id=(partners[r], tile),
            device_id_type=pl.DeviceIdType.MESH,
        )
        copy.start()
        copy.wait()
        last = r == n_rounds - 1
        dst = out_ref if last else acc[r]
        combine_rows(dst, src, bits[r] * half, recv[r], bits[r] == 1, half, last)
        src = dst


def render_composite(density, bins, table, depth_scale, n_rounds):
    planes, rows, width = density.shape
    lane_rounds = 0
    while (width >> (lane_rounds + 1)) >= LANES and lane_rounds < n_rounds:
        lane_rounds += 1
    n_chunks = rows // ROW_BLOCK
    shapes = []
    for r in range(n_rounds):
        half = width >> (r + 1)
        shapes.append((4, rows, half) if r < lane_rounds else (4, half, rows))
    scratch = [
        pltpu.VMEM((4, rows, width), jnp.float32),
        pltpu.VMEM((6, rows, width), jnp.float32),
        pltpu.VMEM((rows, width), jnp.float32),
        pltpu.VMEM((rows, width), jnp.float32),
        pltpu.VMEM((planes, 8, width), jnp.float32),
        pltpu.VMEM((planes, 8, width), jnp.float32),
        pltpu.SemaphoreType.DMA((2 + 2 * n_chunks,)),
        pltpu.SemaphoreType.DMA((2 + 2 * n_chunks,)),
    ]
    scratch += [pltpu.VMEM(s, jnp.float32) for s in shapes]
    scratch += [pltpu.VMEM(s, jnp.float32) for s in shapes[:-1]]
    scratch += [pltpu.VMEM((4, width >> lane_rounds, rows), jnp.float32)]
    n_sems = lane_rounds * n_chunks + n_rounds - lane_rounds
    scratch += [pltpu.SemaphoreType.DMA((n_sems,)), pltpu.SemaphoreType.DMA((n_sems,))]
    scratch += [pltpu.VMEM((4,) + shapes[-1], jnp.float32), pltpu.SemaphoreType.DMA((3,)),
                pltpu.SemaphoreType.DMA((4,))]
    vmem = pl.BlockSpec(memory_space=pltpu.VMEM)
    out = pl.pallas_call(
        functools.partial(fused_kernel, depth_scale, n_rounds, lane_rounds, n_chunks),
        out_shape=jax.ShapeDtypeStruct(shapes[-1], jnp.float32),
        in_specs=[vmem] * 3,
        out_specs=vmem,
        scratch_shapes=scratch,
        compiler_params=pltpu.CompilerParams(
            collective_id=0, has_side_effects=True, vmem_limit_bytes=48 * 1024 * 1024),
    )(table, density, bins)
    return jnp.transpose(out, (0, 2, 1))


def per_device(density, bins, colors, extinction):
    depth_cells = density.shape[0]
    slab_count = lax.axis_size("depth")
    depth_scale = 0.6 / (depth_cells * slab_count)
    lookup = jnp.concatenate([colors, extinction[None, :]], 0).astype(jnp.float32)
    table = jnp.concatenate([lookup, jnp.zeros((4, lookup.shape[1]), jnp.float32)], 0)
    return render_composite(density, bins, table, depth_scale, slab_count.bit_length() - 1)


def solution(mesh):
    return jax.shard_map(
        per_device,
        mesh=mesh,
        in_specs=(P("depth", "tile", None), P("depth", "tile", None), P(), P()),
        out_specs=P(None, "tile", "depth"),
        check_vma=False,
    )
```

```python
import functools

import jax
import jax.numpy as jnp
from jax import lax
from jax.experimental import pallas as pl
from jax.experimental.pallas import tpu as pltpu
from jax.sharding import PartitionSpec as P

ROW_BLOCK = 16
LANES = 128
LOOK_UNROLL = 4
SHADE_UNROLL = 2


def make_look(tables):
    def look(idx):
        low = idx & (LANES - 1)
        high = idx >= LANES
        vals = []
        for lo_t, hi_t in tables:
            lo_v = jnp.take_along_axis(lo_t, low, axis=1, mode="promise_in_bounds")
            hi_v = jnp.take_along_axis(hi_t, low, axis=1, mode="promise_in_bounds")
            vals.append(jnp.where(high, hi_v, lo_v))
        return vals

    return look


def lookup_rows(depth_scale, look, b_ref, stash_ref, img_ref, row0, n_rows):
    groups = b_ref.shape[2] // LANES
    per_step = n_rows // 8

    def body(g, carry):
        col = pl.ds(pl.multiple_of(g * LANES, LANES), LANES)
        for kk in range(per_step):
            r_sl = pl.ds(row0 + kk * 8, 8)
            e0 = look(b_ref[0, r_sl, col])
            e1 = look(b_ref[1, r_sl, col])
            o0 = e0[3] * depth_scale
            o1 = e1[3] * depth_scale
            a0 = 1.0 - jnp.exp(-o0)
            a1 = 1.0 - jnp.exp(-o1)
            t0 = jnp.exp(-o0)
            for ch in range(3):
                stash_ref[ch, r_sl, col] = e0[ch] * a0
                stash_ref[3 + ch, r_sl, col] = t0 * (e1[ch] * a1)
            img_ref[3, r_sl, col] = jnp.exp(-(o0 + o1))
        return carry

    lax.fori_loop(0, groups, body, 0, unroll=LOOK_UNROLL)


def shade_rows(c, n_chunks, d_ref, htop_ref, hbot_ref, xp_ref, xn_ref, has_top, has_bot,
               has_prev, has_next, stash_ref, img_ref):
    row_block = d_ref.shape[1] // n_chunks
    chunks = row_block // 8
    groups = d_ref.shape[2] // LANES
    base = c * row_block
    sub = lax.broadcasted_iota(jnp.int32, (8, LANES), 0)
    lane = lax.broadcasted_iota(jnp.int32, (8, LANES), 1)

    def group_body(g, carry):
        col = pl.ds(pl.multiple_of(g * LANES, LANES), LANES)
        col_l = pl.ds(pl.multiple_of(jnp.maximum(g - 1, 0) * LANES, LANES), LANES)
        col_r = pl.ds(pl.multiple_of(jnp.minimum(g + 1, groups - 1) * LANES, LANES), LANES)
        has_l = g > 0
        has_r = g < groups - 1
        centers = [[d_ref[p, pl.ds(base + k * 8, 8), col] for k in range(chunks)] for p in range(2)]
        for k in range(chunks):
            rows = pl.ds(base + k * 8, 8)
            shades = []
            for p in range(2):
                c_v = centers[p][k]
                if k > 0:
                    up_src = centers[p][k - 1]
                elif c == 0:
                    up_src = jnp.where(has_top, htop_ref[p, :, col], 0.0)
                else:
                    up_src = d_ref[p, pl.ds(base - 8, 8), col]
                if k < chunks - 1:
                    dn_src = centers[p][k + 1]
                elif c == n_chunks - 1:
                    dn_src = jnp.where(has_bot, hbot_ref[p, :, col], 0.0)
                else:
                    dn_src = d_ref[p, pl.ds(base + row_block, 8), col]
                up = jnp.where(sub == 0, pltpu.roll(up_src, 1, 0), pltpu.roll(c_v, 1, 0))
                dn = jnp.where(sub == 7, pltpu.roll(dn_src, 7, 0), pltpu.roll(c_v, 7, 0))
                grad_y = (dn - up) * 0.5
                left_src = jnp.where(has_l, d_ref[p, rows, col_l], 0.0)
                right_src = jnp.where(has_r, d_ref[p, rows, col_r], 0.0)
                lf = jnp.where(lane == 0, pltpu.roll(left_src, 1, 1), pltpu.roll(c_v, 1, 1))
                rt = jnp.where(lane == LANES - 1, pltpu.roll(right_src, LANES - 1, 1),
                               pltpu.roll(c_v, LANES - 1, 1))
                grad_z = (rt - lf) * 0.5
                if p == 0:
                    grad_x = (centers[1][k] - jnp.where(has_prev, xp_ref[rows, col], 0.0)) * 0.5
                else:
                    grad_x = (jnp.where(has_next, xn_ref[rows, col], 0.0) - centers[0][k]) * 0.5
                lit = jnp.abs(0.48 * grad_x + 0.6 * grad_y + 0.64 * grad_z)
                shades.append(0.3 + 0.7 * lit / jnp.sqrt(
                    grad_x * grad_x + grad_y * grad_y + grad_z * grad_z + 1.0))
            for ch in range(3):
                img_ref[ch, rows, col] = (stash_ref[ch, rows, col] * shades[0]
                                          + stash_ref[3 + ch, rows, col] * shades[1])
        return carry

    lax.fori_loop(0, groups, group_body, 0, unroll=SHADE_UNROLL)


def combine_lanes(dst_ref, src_ref, keep_off, rcv_ref, behind, row0, n_rows, half):
    lanes = min(half, LANES)
    groups = half // lanes

    def body(i, carry):
        r_sl = pl.ds(pl.multiple_of(row0 + i * 8, 8), 8)
        for j in range(groups):
            k_sl = pl.ds(pl.multiple_of(keep_off + j * lanes, lanes), lanes)
            d_sl = pl.ds(j * lanes, lanes)
            kept = [src_ref[ch, r_sl, k_sl] for ch in range(4)]
            rcv = [rcv_ref[ch, r_sl, d_sl] for ch in range(4)]
            front = [jnp.where(behind, q, k) for k, q in zip(kept, rcv)]
            back = [jnp.where(behind, k, q) for k, q in zip(kept, rcv)]
            for ch in range(3):
                dst_ref[ch, r_sl, d_sl] = front[ch] + front[3] * back[ch]
            dst_ref[3, r_sl, d_sl] = front[3] * back[3]
        return carry

    lax.fori_loop(0, n_rows // 8, body, 0)


def combine_rows(dst_ref, src_ref, keep_off, rcv_ref, behind, half, finish):
    def body(i, carry):
        r_k = pl.ds(pl.multiple_of(keep_off + i * 8, 8), 8)
        r_d = pl.ds(pl.multiple_of(i * 8, 8), 8)
        kept = [src_ref[ch, r_k, :] for ch in range(4)]
        rcv = [rcv_ref[ch, r_d, :] for ch in range(4)]
        front = [jnp.where(behind, q, k) for k, q in zip(kept, rcv)]
        back = [jnp.where(behind, k, q) for k, q in zip(kept, rcv)]
        for ch in range(3):
            dst_ref[ch, r_d, :] = front[ch] + front[3] * back[ch]
        trans = front[3] * back[3]
        dst_ref[3, r_d, :] = (1.0 - trans) if finish else trans
        return carry

    lax.fori_loop(0, half // 8, body, 0)


def fused_kernel(depth_scale, n_rounds, lane_rounds, n_chunks, table_ref, d_ref, b_ref, out_ref,
                 img_ref, stash_ref, xp_ref, xn_ref, htop_ref, hbot_ref, halo_send, halo_recv, *scratch):
    recv = scratch[:n_rounds]
    acc = scratch[n_rounds:2 * n_rounds - 1]
    flip_ref = scratch[2 * n_rounds - 1]
    send_sems, recv_sems, parts_ref, tail_send, tail_recv, y_parts, y_send, y_recv = scratch[2 * n_rounds:]
    me = lax.axis_index("depth")
    tile = lax.axis_index("tile")
    n_slabs = lax.axis_size("depth")
    n_tiles = lax.axis_size("tile")
    bits = [(me // (1 << r)) % 2 for r in range(n_rounds)]
    partners = [me + (1 - 2 * bits[r]) * (1 << r) for r in range(n_rounds)]
    rows = d_ref.shape[1]
    width = d_ref.shape[2]
    row_block = rows // n_chunks
    halves = [width >> (r + 1) for r in range(n_rounds)]
    srcs = [img_ref] + list(acc)
    mesh_id = pl.DeviceIdType.MESH
    has_prev = me > 0
    has_next = me < n_slabs - 1
    has_top = tile > 0
    has_bot = tile < n_tiles - 1
    odd = bits[0] == 1
    extra_nb = jnp.where(odd, has_next, has_prev)
    extra_id = jnp.where(odd, me + 1, me - 1)

    barrier = pltpu.get_barrier_semaphore()
    for r in range(n_rounds):
        pl.semaphore_signal(barrier, inc=1, device_id=(partners[r], tile), device_id_type=mesh_id)

    @pl.when(extra_nb)
    def _():
        pl.semaphore_signal(barrier, inc=1, device_id=(extra_id, tile), device_id_type=mesh_id)

    @pl.when(has_top)
    def _():
        pl.semaphore_signal(barrier, inc=1, device_id=(me, tile - 1), device_id_type=mesh_id)

    @pl.when(has_bot)
    def _():
        pl.semaphore_signal(barrier, inc=1, device_id=(me, tile + 1), device_id_type=mesh_id)

    direct = n_rounds - lane_rounds == 2
    group_step = 1 << lane_rounds
    member = (me // group_step) % 4
    group_base = me - member * group_step
    if direct:
        pl.semaphore_signal(barrier, inc=1, device_id=(group_base + (3 - member) * group_step, tile),
                            device_id_type=mesh_id)
    y_direct = lane_rounds >= 3
    y_member = (me // 2) % 4
    y_base = me - y_member * 2
    if y_direct:
        pl.semaphore_signal(barrier, inc=1, device_id=(y_base + (3 - y_member) * 2, tile),
                            device_id_type=mesh_id)
    n_greet = (n_rounds + int(direct) + int(y_direct) + extra_nb.astype(jnp.int32) + has_top.astype(jnp.int32)
               + has_bot.astype(jnp.int32))
    pl.semaphore_wait(barrier, n_greet)

    def halo(send_if, recv_if, src_ref, dst_ref, idx, dev):
        return (send_if, recv_if, pltpu.make_async_remote_copy(
            src_ref=src_ref, dst_ref=dst_ref, send_sem=halo_send.at[idx],
            recv_sem=halo_recv.at[idx], device_id=dev, device_id_type=mesh_id))

    edge_copies = [
        halo(has_bot, has_top, d_ref.at[:, pl.ds(rows - 8, 8), :], htop_ref, 0, (me, tile + 1)),
        halo(has_top, has_bot, d_ref.at[:, pl.ds(0, 8), :], hbot_ref, 1, (me, tile - 1)),
    ]
    plane_copies = []
    for c in range(n_chunks):
        row_sl = pl.ds(c * row_block, row_block)
        plane_copies.append((
            halo(has_next, has_prev, d_ref.at[1, row_sl, :], xp_ref.at[row_sl, :], 2 + 2 * c,
                 (me + 1, tile)),
            halo(has_prev, has_next, d_ref.at[0, row_sl, :], xn_ref.at[row_sl, :], 3 + 2 * c,
                 (me - 1, tile)),
        ))
    all_halos = edge_copies + [h for pair in plane_copies for h in pair]
    for send_if, _, copy in all_halos:
        pl.when(send_if)(copy.start)

    tables = [
        (jnp.broadcast_to(table_ref[ch:ch + 1, 0:LANES], (8, LANES)),
         jnp.broadcast_to(table_ref[ch:ch + 1, LANES:2 * LANES], (8, LANES)))
        for ch in range(4)
    ]
    look = make_look(tables)
    copies = {}

    def start_lane(r, c):
        row_sl = pl.ds(c * row_block, row_block)
        send_off = pl.multiple_of((1 - bits[r]) * halves[r], LANES)
        copy = pltpu.make_async_remote_copy(
            src_ref=srcs[r].at[:, row_sl, pl.ds(send_off, halves[r])],
            dst_ref=recv[r].at[:, row_sl, :],
            send_sem=send_sems.at[r * n_chunks + c],
            recv_sem=recv_sems.at[r * n_chunks + c],
            device_id=(partners[r], tile),
            device_id_type=pl.DeviceIdType.MESH,
        )
        copy.start()
        copies[(r, c)] = copy

    y_quarter = halves[2]

    def y_owned(j):
        return (j % 2) * halves[1] + (j // 2) * y_quarter

    y_sends = []

    def start_y(c):
        row_sl = pl.ds(c * row_block, row_block)
        for k in range(1, 4):
            dst_j = (y_member + k) % 4
            copy = pltpu.make_async_remote_copy(
                src_ref=acc[0].at[:, row_sl, pl.ds(pl.multiple_of(y_owned(dst_j), LANES), y_quarter)],
                dst_ref=y_parts.at[y_member, :, row_sl, :],
                send_sem=y_send.at[(k - 1) * n_chunks + c],
                recv_sem=y_recv.at[y_member * n_chunks + c],
                device_id=(y_base + dst_j * 2, tile),
                device_id_type=mesh_id,
            )
            copy.start()
            y_sends.append(copy)

    def finish_y(c):
        row_sl = pl.ds(c * row_block, row_block)
        for k in range(1, 4):
            src_j = (y_member + 4 - k) % 4
            pltpu.make_async_remote_copy(
                src_ref=acc[0].at[:, row_sl, pl.ds(0, y_quarter)],
                dst_ref=y_parts.at[src_j, :, row_sl, :],
                send_sem=y_send.at[(k - 1) * n_chunks + c],
                recv_sem=y_recv.at[src_j * n_chunks + c],
                device_id=(y_base + src_j * 2, tile),
                device_id_type=mesh_id,
            ).wait_recv()
        own = pl.multiple_of(y_owned(y_member), LANES)

        def body(i, carry):
            r_sl = pl.ds(pl.multiple_of(c * row_block + i * 8, 8), 8)
            for g in range(y_quarter // LANES):
                col = pl.ds(g * LANES, LANES)
                own_col = pl.ds(pl.multiple_of(own + g * LANES, LANES), LANES)
                parts = []
                for j in range(4):
                    mine = [acc[0][ch, r_sl, own_col] for ch in range(4)]
                    got = [y_parts[j, ch, r_sl, col] for ch in range(4)]
                    parts.append([jnp.where(y_member == j, m, q) for m, q in zip(mine, got)])
                front = parts[0]
                for back in parts[1:]:
                    front = ([front[ch] + front[3] * back[ch] for ch in range(3)]
                             + [front[3] * back[3]])
                for ch in range(4):
                    acc[2][ch, r_sl, col] = front[ch]
            return carry

        lax.fori_loop(0, row_block // 8, body, 0)
        if lane_rounds > 3:
            start_lane(3, c)

    def finish_lane(r, c):
        copies[(r, c)].wait()
        combine_lanes(acc[r], srcs[r], bits[r] * halves[r], recv[r], bits[r] == 1,
                      c * row_block, row_block, halves[r])
        if y_direct and r == 0:
            start_y(c)
        elif r + 1 < lane_rounds:
            start_lane(r + 1, c)

    for c in range(n_chunks):
        lookup_rows(depth_scale, look, b_ref, stash_ref, img_ref, c * row_block, row_block)
        waits = list(plane_copies[c])
        if c == 0:
            waits.append(edge_copies[0])
        if c == n_chunks - 1:
            waits.append(edge_copies[1])
        for _, recv_if, copy in waits:
            pl.when(recv_if)(copy.wait_recv)
        shade_rows(c, n_chunks, d_ref, htop_ref, hbot_ref, xp_ref, xn_ref, has_top, has_bot,
                   has_prev, has_next, stash_ref, img_ref)
        start_lane(0, c)
        if c >= 1:
            finish_lane(0, c - 1)
    finish_lane(0, n_chunks - 1)
    for r in range(1, lane_rounds):
        for c in range(n_chunks):
            if y_direct and r == 1:
                finish_y(c)
            elif y_direct and r == 2:
                continue
            else:
                finish_lane(r, c)
    for copy in y_sends:
        copy.wait_send()
    for send_if, _, copy in all_halos:
        pl.when(send_if)(copy.wait_send)

    src = acc[lane_rounds - 1]
    for ch in range(4):
        flip_ref[ch] = src[ch].T
    src = flip_ref
    if direct:
        quarter = halves[-1]

        def owned(j):
            return (2 * (j % 2) + j // 2) * quarter

        sends = []
        for k in range(1, 4):
            dst_j = (member + k) % 4
            copy = pltpu.make_async_remote_copy(
                src_ref=flip_ref.at[:, pl.ds(pl.multiple_of(owned(dst_j), 8), quarter), :],
                dst_ref=parts_ref.at[member],
                send_sem=tail_send.at[k - 1],
                recv_sem=tail_recv.at[member],
                device_id=(group_base + dst_j * group_step, tile),
                device_id_type=mesh_id,
            )
            copy.start()
            sends.append(copy)
        parts_ref[member] = flip_ref[:, pl.ds(pl.multiple_of(owned(member), 8), quarter), :]
        for k in range(1, 4):
            src_j = (member + 4 - k) % 4
            pltpu.make_async_remote_copy(
                src_ref=flip_ref.at[:, pl.ds(0, quarter), :],
                dst_ref=parts_ref.at[src_j],
                send_sem=tail_send.at[k - 1],
                recv_sem=tail_recv.at[src_j],
                device_id=(group_base + src_j * group_step, tile),
                device_id_type=mesh_id,
            ).wait_recv()
        for copy in sends:
            copy.wait_send()
        front = [parts_ref[0, ch] for ch in range(4)]
        for j in range(1, 4):
            back = [parts_ref[j, ch] for ch in range(4)]
            front = [front[ch] + front[3] * back[ch] for ch in range(3)] + [front[3] * back[3]]
        for ch in range(3):
            out_ref[ch] = front[ch]
        out_ref[3] = 1.0 - front[3]
        return

    sem_base = lane_rounds * n_chunks
    for r in range(lane_rounds, n_rounds):
        half = halves[r]
        send_off = pl.multiple_of((1 - bits[r]) * half, 8)
        copy = pltpu.make_async_remote_copy(
            src_ref=src.at[:, pl.ds(send_off, half), :],
            dst_ref=recv[r],
            send_sem=send_sems.at[sem_base + r - lane_rounds],
            recv_sem=recv_sems.at[sem_base + r - lane_rounds],
            device_id=(partners[r], tile),
            device_id_type=pl.DeviceIdType.MESH,
        )
        copy.start()
        copy.wait()
        last = r == n_rounds - 1
        dst = out_ref if last else acc[r]
        combine_rows(dst, src, bits[r] * half, recv[r], bits[r] == 1, half, last)
        src = dst


def render_composite(density, bins, table, depth_scale, n_rounds):
    planes, rows, width = density.shape
    lane_rounds = 0
    while (width >> (lane_rounds + 1)) >= LANES and lane_rounds < n_rounds:
        lane_rounds += 1
    n_chunks = rows // ROW_BLOCK
    shapes = []
    for r in range(n_rounds):
        half = width >> (r + 1)
        shapes.append((4, rows, half) if r < lane_rounds else (4, half, rows))
    scratch = [
        pltpu.VMEM((4, rows, width), jnp.float32),
        pltpu.VMEM((6, rows, width), jnp.float32),
        pltpu.VMEM((rows, width), jnp.float32),
        pltpu.VMEM((rows, width), jnp.float32),
        pltpu.VMEM((planes, 8, width), jnp.float32),
        pltpu.VMEM((planes, 8, width), jnp.float32),
        pltpu.SemaphoreType.DMA((2 + 2 * n_chunks,)),
        pltpu.SemaphoreType.DMA((2 + 2 * n_chunks,)),
    ]
    scratch += [pltpu.VMEM(s, jnp.float32) for s in shapes]
    scratch += [pltpu.VMEM(s, jnp.float32) for s in shapes[:-1]]
    scratch += [pltpu.VMEM((4, width >> lane_rounds, rows), jnp.float32)]
    n_sems = lane_rounds * n_chunks + n_rounds - lane_rounds
    scratch += [pltpu.SemaphoreType.DMA((n_sems,)), pltpu.SemaphoreType.DMA((n_sems,))]
    scratch += [pltpu.VMEM((4,) + shapes[-1], jnp.float32), pltpu.SemaphoreType.DMA((3,)),
                pltpu.SemaphoreType.DMA((4,))]
    y_quarter = width >> 3
    scratch += [pltpu.VMEM((4, 4, rows, y_quarter), jnp.float32),
                pltpu.SemaphoreType.DMA((3 * n_chunks,)), pltpu.SemaphoreType.DMA((4 * n_chunks,))]
    vmem = pl.BlockSpec(memory_space=pltpu.VMEM)
    out = pl.pallas_call(
        functools.partial(fused_kernel, depth_scale, n_rounds, lane_rounds, n_chunks),
        out_shape=jax.ShapeDtypeStruct(shapes[-1], jnp.float32),
        in_specs=[vmem] * 3,
        out_specs=vmem,
        scratch_shapes=scratch,
        compiler_params=pltpu.CompilerParams(
            collective_id=0, has_side_effects=True, vmem_limit_bytes=48 * 1024 * 1024),
    )(table, density, bins)
    return jnp.transpose(out, (0, 2, 1))


def per_device(density, bins, colors, extinction):
    depth_cells = density.shape[0]
    slab_count = lax.axis_size("depth")
    depth_scale = 0.6 / (depth_cells * slab_count)
    lookup = jnp.concatenate([colors, extinction[None, :]], 0).astype(jnp.float32)
    table = jnp.concatenate([lookup, jnp.zeros((4, lookup.shape[1]), jnp.float32)], 0)
    return render_composite(density, bins, table, depth_scale, slab_count.bit_length() - 1)


def solution(mesh):
    return jax.shard_map(
        per_device,
        mesh=mesh,
        in_specs=(P("depth", "tile", None), P("depth", "tile", None), P(), P()),
        out_specs=P(None, "tile", "depth"),
        check_vma=False,
    )
```

```python
import functools

import jax
import jax.numpy as jnp
from jax import lax
from jax.experimental import pallas as pl
from jax.experimental.pallas import tpu as pltpu
from jax.sharding import PartitionSpec as P

ROW_BLOCK = 16
LANES = 128
LOOK_UNROLL = 4
SHADE_UNROLL = 2


def make_look(tables):
    def look(idx):
        low = idx & (LANES - 1)
        high = idx >= LANES
        vals = []
        for lo_t, hi_t in tables:
            lo_v = jnp.take_along_axis(lo_t, low, axis=1, mode="promise_in_bounds")
            hi_v = jnp.take_along_axis(hi_t, low, axis=1, mode="promise_in_bounds")
            vals.append(jnp.where(high, hi_v, lo_v))
        return vals

    return look


def lookup_rows(depth_scale, look, b_ref, stash_ref, img_ref, row0, n_rows):
    groups = b_ref.shape[2] // LANES
    per_step = n_rows // 8

    def body(g, carry):
        col = pl.ds(pl.multiple_of(g * LANES, LANES), LANES)
        for kk in range(per_step):
            r_sl = pl.ds(row0 + kk * 8, 8)
            e0 = look(b_ref[0, r_sl, col])
            e1 = look(b_ref[1, r_sl, col])
            o0 = e0[3] * depth_scale
            o1 = e1[3] * depth_scale
            a0 = 1.0 - jnp.exp(-o0)
            a1 = 1.0 - jnp.exp(-o1)
            t0 = jnp.exp(-o0)
            for ch in range(3):
                stash_ref[ch, r_sl, col] = e0[ch] * a0
                stash_ref[3 + ch, r_sl, col] = t0 * (e1[ch] * a1)
            img_ref[3, r_sl, col] = jnp.exp(-(o0 + o1))
        return carry

    lax.fori_loop(0, groups, body, 0, unroll=LOOK_UNROLL)


def shade_rows(c, n_chunks, d_ref, htop_ref, hbot_ref, xp_ref, xn_ref, has_top, has_bot,
               has_prev, has_next, stash_ref, img_ref):
    row_block = d_ref.shape[1] // n_chunks
    chunks = row_block // 8
    groups = d_ref.shape[2] // LANES
    base = c * row_block
    sub = lax.broadcasted_iota(jnp.int32, (8, LANES), 0)
    lane = lax.broadcasted_iota(jnp.int32, (8, LANES), 1)

    def group_body(g, carry):
        col = pl.ds(pl.multiple_of(g * LANES, LANES), LANES)
        col_l = pl.ds(pl.multiple_of(jnp.maximum(g - 1, 0) * LANES, LANES), LANES)
        col_r = pl.ds(pl.multiple_of(jnp.minimum(g + 1, groups - 1) * LANES, LANES), LANES)
        has_l = g > 0
        has_r = g < groups - 1
        centers = [[d_ref[p, pl.ds(base + k * 8, 8), col] for k in range(chunks)] for p in range(2)]
        for k in range(chunks):
            rows = pl.ds(base + k * 8, 8)
            shades = []
            for p in range(2):
                c_v = centers[p][k]
                if k > 0:
                    up_src = centers[p][k - 1]
                elif c == 0:
                    up_src = jnp.where(has_top, htop_ref[p, :, col], 0.0)
                else:
                    up_src = d_ref[p, pl.ds(base - 8, 8), col]
                if k < chunks - 1:
                    dn_src = centers[p][k + 1]
                elif c == n_chunks - 1:
                    dn_src = jnp.where(has_bot, hbot_ref[p, :, col], 0.0)
                else:
                    dn_src = d_ref[p, pl.ds(base + row_block, 8), col]
                up = jnp.where(sub == 0, pltpu.roll(up_src, 1, 0), pltpu.roll(c_v, 1, 0))
                dn = jnp.where(sub == 7, pltpu.roll(dn_src, 7, 0), pltpu.roll(c_v, 7, 0))
                grad_y = (dn - up) * 0.5
                left_src = jnp.where(has_l, d_ref[p, rows, col_l], 0.0)
                right_src = jnp.where(has_r, d_ref[p, rows, col_r], 0.0)
                lf = jnp.where(lane == 0, pltpu.roll(left_src, 1, 1), pltpu.roll(c_v, 1, 1))
                rt = jnp.where(lane == LANES - 1, pltpu.roll(right_src, LANES - 1, 1),
                               pltpu.roll(c_v, LANES - 1, 1))
                grad_z = (rt - lf) * 0.5
                if p == 0:
                    grad_x = (centers[1][k] - jnp.where(has_prev, xp_ref[rows, col], 0.0)) * 0.5
                else:
                    grad_x = (jnp.where(has_next, xn_ref[rows, col], 0.0) - centers[0][k]) * 0.5
                lit = jnp.abs(0.48 * grad_x + 0.6 * grad_y + 0.64 * grad_z)
                shades.append(0.3 + 0.7 * lit / jnp.sqrt(
                    grad_x * grad_x + grad_y * grad_y + grad_z * grad_z + 1.0))
            for ch in range(3):
                img_ref[ch, rows, col] = (stash_ref[ch, rows, col] * shades[0]
                                          + stash_ref[3 + ch, rows, col] * shades[1])
        return carry

    lax.fori_loop(0, groups, group_body, 0, unroll=SHADE_UNROLL)


def combine_lanes(dst_ref, src_ref, keep_off, rcv_ref, behind, row0, n_rows, half):
    lanes = min(half, LANES)
    groups = half // lanes

    def body(i, carry):
        r_sl = pl.ds(pl.multiple_of(row0 + i * 8, 8), 8)
        for j in range(groups):
            k_sl = pl.ds(pl.multiple_of(keep_off + j * lanes, lanes), lanes)
            d_sl = pl.ds(j * lanes, lanes)
            kept = [src_ref[ch, r_sl, k_sl] for ch in range(4)]
            rcv = [rcv_ref[ch, r_sl, d_sl] for ch in range(4)]
            front = [jnp.where(behind, q, k) for k, q in zip(kept, rcv)]
            back = [jnp.where(behind, k, q) for k, q in zip(kept, rcv)]
            for ch in range(3):
                dst_ref[ch, r_sl, d_sl] = front[ch] + front[3] * back[ch]
            dst_ref[3, r_sl, d_sl] = front[3] * back[3]
        return carry

    lax.fori_loop(0, n_rows // 8, body, 0)


def combine_rows(dst_ref, src_ref, keep_off, rcv_ref, behind, half, finish):
    def body(i, carry):
        r_k = pl.ds(pl.multiple_of(keep_off + i * 8, 8), 8)
        r_d = pl.ds(pl.multiple_of(i * 8, 8), 8)
        kept = [src_ref[ch, r_k, :] for ch in range(4)]
        rcv = [rcv_ref[ch, r_d, :] for ch in range(4)]
        front = [jnp.where(behind, q, k) for k, q in zip(kept, rcv)]
        back = [jnp.where(behind, k, q) for k, q in zip(kept, rcv)]
        for ch in range(3):
            dst_ref[ch, r_d, :] = front[ch] + front[3] * back[ch]
        trans = front[3] * back[3]
        dst_ref[3, r_d, :] = (1.0 - trans) if finish else trans
        return carry

    lax.fori_loop(0, half // 8, body, 0)


def fused_kernel(depth_scale, n_rounds, lane_rounds, n_chunks, colors_ref, ext_ref, d_hbm, b_hbm,
                 out_ref, d_ref, b_ref, load_sems, img_ref, stash_ref, xp_ref, xn_ref, htop_ref, hbot_ref,
                 halo_send, halo_recv, *scratch):
    recv = scratch[:n_rounds]
    acc = scratch[n_rounds:2 * n_rounds - 1]
    flip_ref = scratch[2 * n_rounds - 1]
    send_sems, recv_sems, parts_ref, tail_send, tail_recv, y_parts, y_send, y_recv = scratch[2 * n_rounds:]
    me = lax.axis_index("depth")
    tile = lax.axis_index("tile")
    n_slabs = lax.axis_size("depth")
    n_tiles = lax.axis_size("tile")
    bits = [(me // (1 << r)) % 2 for r in range(n_rounds)]
    partners = [me + (1 - 2 * bits[r]) * (1 << r) for r in range(n_rounds)]
    rows = d_ref.shape[1]
    width = d_ref.shape[2]
    row_block = rows // n_chunks
    halves = [width >> (r + 1) for r in range(n_rounds)]
    srcs = [img_ref] + list(acc)
    mesh_id = pl.DeviceIdType.MESH
    has_prev = me > 0
    has_next = me < n_slabs - 1
    has_top = tile > 0
    has_bot = tile < n_tiles - 1
    odd = bits[0] == 1
    extra_nb = jnp.where(odd, has_next, has_prev)
    extra_id = jnp.where(odd, me + 1, me - 1)

    loads = []
    for c in range(n_chunks):
        row_sl = pl.ds(c * row_block, row_block)
        pair = (pltpu.make_async_copy(d_hbm.at[:, row_sl, :], d_ref.at[:, row_sl, :],
                                      load_sems.at[2 * c]),
                pltpu.make_async_copy(b_hbm.at[:, row_sl, :], b_ref.at[:, row_sl, :],
                                      load_sems.at[2 * c + 1]))
        for copy in pair:
            copy.start()
        loads.append(pair)

    barrier = pltpu.get_barrier_semaphore()
    for r in range(n_rounds):
        pl.semaphore_signal(barrier, inc=1, device_id=(partners[r], tile), device_id_type=mesh_id)

    @pl.when(extra_nb)
    def _():
        pl.semaphore_signal(barrier, inc=1, device_id=(extra_id, tile), device_id_type=mesh_id)

    @pl.when(has_top)
    def _():
        pl.semaphore_signal(barrier, inc=1, device_id=(me, tile - 1), device_id_type=mesh_id)

    @pl.when(has_bot)
    def _():
        pl.semaphore_signal(barrier, inc=1, device_id=(me, tile + 1), device_id_type=mesh_id)

    direct = n_rounds - lane_rounds == 2
    group_step = 1 << lane_rounds
    member = (me // group_step) % 4
    group_base = me - member * group_step
    if direct:
        pl.semaphore_signal(barrier, inc=1, device_id=(group_base + (3 - member) * group_step, tile),
                            device_id_type=mesh_id)
    y_direct = lane_rounds >= 3
    y_member = (me // 2) % 4
    y_base = me - y_member * 2
    if y_direct:
        pl.semaphore_signal(barrier, inc=1, device_id=(y_base + (3 - y_member) * 2, tile),
                            device_id_type=mesh_id)
    n_greet = (n_rounds + int(direct) + int(y_direct) + extra_nb.astype(jnp.int32) + has_top.astype(jnp.int32)
               + has_bot.astype(jnp.int32))
    pl.semaphore_wait(barrier, n_greet)

    def halo(send_if, recv_if, src_ref, dst_ref, idx, dev):
        return (send_if, recv_if, pltpu.make_async_remote_copy(
            src_ref=src_ref, dst_ref=dst_ref, send_sem=halo_send.at[idx],
            recv_sem=halo_recv.at[idx], device_id=dev, device_id_type=mesh_id))

    edge_copies = [
        halo(has_bot, has_top, d_hbm.at[:, pl.ds(rows - 8, 8), :], htop_ref, 0, (me, tile + 1)),
        halo(has_top, has_bot, d_hbm.at[:, pl.ds(0, 8), :], hbot_ref, 1, (me, tile - 1)),
    ]
    plane_copies = []
    for c in range(n_chunks):
        row_sl = pl.ds(c * row_block, row_block)
        plane_copies.append((
            halo(has_next, has_prev, d_hbm.at[1, row_sl, :], xp_ref.at[row_sl, :], 2 + 2 * c,
                 (me + 1, tile)),
            halo(has_prev, has_next, d_hbm.at[0, row_sl, :], xn_ref.at[row_sl, :], 3 + 2 * c,
                 (me - 1, tile)),
        ))
    all_halos = edge_copies + [h for pair in plane_copies for h in pair]
    for send_if, _, copy in all_halos:
        pl.when(send_if)(copy.start)

    lookup = jnp.concatenate([colors_ref[...].astype(jnp.float32),
                              ext_ref[...].astype(jnp.float32)], 0)
    tables = [
        (jnp.broadcast_to(lookup[ch:ch + 1, 0:LANES], (8, LANES)),
         jnp.broadcast_to(lookup[ch:ch + 1, LANES:2 * LANES], (8, LANES)))
        for ch in range(4)
    ]
    look = make_look(tables)
    copies = {}

    def start_lane(r, c):
        row_sl = pl.ds(c * row_block, row_block)
        send_off = pl.multiple_of((1 - bits[r]) * halves[r], LANES)
        copy = pltpu.make_async_remote_copy(
            src_ref=srcs[r].at[:, row_sl, pl.ds(send_off, halves[r])],
            dst_ref=recv[r].at[:, row_sl, :],
            send_sem=send_sems.at[r * n_chunks + c],
            recv_sem=recv_sems.at[r * n_chunks + c],
            device_id=(partners[r], tile),
            device_id_type=pl.DeviceIdType.MESH,
        )
        copy.start()
        copies[(r, c)] = copy

    y_quarter = halves[2]

    def y_owned(j):
        return (j % 2) * halves[1] + (j // 2) * y_quarter

    y_sends = []

    def start_y(c):
        row_sl = pl.ds(c * row_block, row_block)
        for k in range(1, 4):
            dst_j = (y_member + k) % 4
            copy = pltpu.make_async_remote_copy(
                src_ref=acc[0].at[:, row_sl, pl.ds(pl.multiple_of(y_owned(dst_j), LANES), y_quarter)],
                dst_ref=y_parts.at[y_member, :, row_sl, :],
                send_sem=y_send.at[(k - 1) * n_chunks + c],
                recv_sem=y_recv.at[y_member * n_chunks + c],
                device_id=(y_base + dst_j * 2, tile),
                device_id_type=mesh_id,
            )
            copy.start()
            y_sends.append(copy)

    def finish_y(c):
        row_sl = pl.ds(c * row_block, row_block)
        for k in range(1, 4):
            src_j = (y_member + 4 - k) % 4
            pltpu.make_async_remote_copy(
                src_ref=acc[0].at[:, row_sl, pl.ds(0, y_quarter)],
                dst_ref=y_parts.at[src_j, :, row_sl, :],
                send_sem=y_send.at[(k - 1) * n_chunks + c],
                recv_sem=y_recv.at[src_j * n_chunks + c],
                device_id=(y_base + src_j * 2, tile),
                device_id_type=mesh_id,
            ).wait_recv()
        own = pl.multiple_of(y_owned(y_member), LANES)

        def body(i, carry):
            r_sl = pl.ds(pl.multiple_of(c * row_block + i * 8, 8), 8)
            for g in range(y_quarter // LANES):
                col = pl.ds(g * LANES, LANES)
                own_col = pl.ds(pl.multiple_of(own + g * LANES, LANES), LANES)
                parts = []
                for j in range(4):
                    mine = [acc[0][ch, r_sl, own_col] for ch in range(4)]
                    got = [y_parts[j, ch, r_sl, col] for ch in range(4)]
                    parts.append([jnp.where(y_member == j, m, q) for m, q in zip(mine, got)])
                front = parts[0]
                for back in parts[1:]:
                    front = ([front[ch] + front[3] * back[ch] for ch in range(3)]
                             + [front[3] * back[3]])
                for ch in range(4):
                    acc[2][ch, r_sl, col] = front[ch]
            return carry

        lax.fori_loop(0, row_block // 8, body, 0)
        if lane_rounds > 3:
            start_lane(3, c)

    def finish_lane(r, c):
        copies[(r, c)].wait()
        combine_lanes(acc[r], srcs[r], bits[r] * halves[r], recv[r], bits[r] == 1,
                      c * row_block, row_block, halves[r])
        if y_direct and r == 0:
            start_y(c)
        elif r + 1 < lane_rounds:
            start_lane(r + 1, c)

    for c in range(n_chunks):
        loads[c][1].wait()
        if c == 0:
            loads[0][0].wait()
        if c + 1 < n_chunks:
            loads[c + 1][0].wait()
        lookup_rows(depth_scale, look, b_ref, stash_ref, img_ref, c * row_block, row_block)
        waits = list(plane_copies[c])
        if c == 0:
            waits.append(edge_copies[0])
        if c == n_chunks - 1:
            waits.append(edge_copies[1])
        for _, recv_if, copy in waits:
            pl.when(recv_if)(copy.wait_recv)
        shade_rows(c, n_chunks, d_ref, htop_ref, hbot_ref, xp_ref, xn_ref, has_top, has_bot,
                   has_prev, has_next, stash_ref, img_ref)
        start_lane(0, c)
        if c >= 1:
            finish_lane(0, c - 1)
    finish_lane(0, n_chunks - 1)
    for r in range(1, lane_rounds):
        for c in range(n_chunks):
            if y_direct and r == 1:
                finish_y(c)
            elif y_direct and r == 2:
                continue
            else:
                finish_lane(r, c)
    for copy in y_sends:
        copy.wait_send()
    for send_if, _, copy in all_halos:
        pl.when(send_if)(copy.wait_send)

    src = acc[lane_rounds - 1]
    for ch in range(4):
        flip_ref[ch] = src[ch].T
    src = flip_ref
    if direct:
        quarter = halves[-1]

        def owned(j):
            return (2 * (j % 2) + j // 2) * quarter

        sends = []
        for k in range(1, 4):
            dst_j = (member + k) % 4
            copy = pltpu.make_async_remote_copy(
                src_ref=flip_ref.at[:, pl.ds(pl.multiple_of(owned(dst_j), 8), quarter), :],
                dst_ref=parts_ref.at[member],
                send_sem=tail_send.at[k - 1],
                recv_sem=tail_recv.at[member],
                device_id=(group_base + dst_j * group_step, tile),
                device_id_type=mesh_id,
            )
            copy.start()
            sends.append(copy)
        parts_ref[member] = flip_ref[:, pl.ds(pl.multiple_of(owned(member), 8), quarter), :]
        for k in range(1, 4):
            src_j = (member + 4 - k) % 4
            pltpu.make_async_remote_copy(
                src_ref=flip_ref.at[:, pl.ds(0, quarter), :],
                dst_ref=parts_ref.at[src_j],
                send_sem=tail_send.at[k - 1],
                recv_sem=tail_recv.at[src_j],
                device_id=(group_base + src_j * group_step, tile),
                device_id_type=mesh_id,
            ).wait_recv()
        for copy in sends:
            copy.wait_send()
        front = [parts_ref[0, ch] for ch in range(4)]
        for j in range(1, 4):
            back = [parts_ref[j, ch] for ch in range(4)]
            front = [front[ch] + front[3] * back[ch] for ch in range(3)] + [front[3] * back[3]]
        for ch in range(3):
            out_ref[ch] = front[ch]
        out_ref[3] = 1.0 - front[3]
        return

    sem_base = lane_rounds * n_chunks
    for r in range(lane_rounds, n_rounds):
        half = halves[r]
        send_off = pl.multiple_of((1 - bits[r]) * half, 8)
        copy = pltpu.make_async_remote_copy(
            src_ref=src.at[:, pl.ds(send_off, half), :],
            dst_ref=recv[r],
            send_sem=send_sems.at[sem_base + r - lane_rounds],
            recv_sem=recv_sems.at[sem_base + r - lane_rounds],
            device_id=(partners[r], tile),
            device_id_type=pl.DeviceIdType.MESH,
        )
        copy.start()
        copy.wait()
        last = r == n_rounds - 1
        dst = out_ref if last else acc[r]
        combine_rows(dst, src, bits[r] * half, recv[r], bits[r] == 1, half, last)
        src = dst


def render_composite(density, bins, colors, extinction, depth_scale, n_rounds):
    planes, rows, width = density.shape
    lane_rounds = 0
    while (width >> (lane_rounds + 1)) >= LANES and lane_rounds < n_rounds:
        lane_rounds += 1
    n_chunks = rows // ROW_BLOCK
    shapes = []
    for r in range(n_rounds):
        half = width >> (r + 1)
        shapes.append((4, rows, half) if r < lane_rounds else (4, half, rows))
    scratch = [
        pltpu.VMEM((planes, rows, width), jnp.float32),
        pltpu.VMEM((planes, rows, width), jnp.int32),
        pltpu.SemaphoreType.DMA((2 * n_chunks,)),
        pltpu.VMEM((4, rows, width), jnp.float32),
        pltpu.VMEM((6, rows, width), jnp.float32),
        pltpu.VMEM((rows, width), jnp.float32),
        pltpu.VMEM((rows, width), jnp.float32),
        pltpu.VMEM((planes, 8, width), jnp.float32),
        pltpu.VMEM((planes, 8, width), jnp.float32),
        pltpu.SemaphoreType.DMA((2 + 2 * n_chunks,)),
        pltpu.SemaphoreType.DMA((2 + 2 * n_chunks,)),
    ]
    scratch += [pltpu.VMEM(s, jnp.float32) for s in shapes]
    scratch += [pltpu.VMEM(s, jnp.float32) for s in shapes[:-1]]
    scratch += [pltpu.VMEM((4, width >> lane_rounds, rows), jnp.float32)]
    n_sems = lane_rounds * n_chunks + n_rounds - lane_rounds
    scratch += [pltpu.SemaphoreType.DMA((n_sems,)), pltpu.SemaphoreType.DMA((n_sems,))]
    scratch += [pltpu.VMEM((4,) + shapes[-1], jnp.float32), pltpu.SemaphoreType.DMA((3,)),
                pltpu.SemaphoreType.DMA((4,))]
    y_quarter = width >> 3
    scratch += [pltpu.VMEM((4, 4, rows, y_quarter), jnp.float32),
                pltpu.SemaphoreType.DMA((3 * n_chunks,)), pltpu.SemaphoreType.DMA((4 * n_chunks,))]
    vmem = pl.BlockSpec(memory_space=pltpu.VMEM)
    out = pl.pallas_call(
        functools.partial(fused_kernel, depth_scale, n_rounds, lane_rounds, n_chunks),
        out_shape=jax.ShapeDtypeStruct(shapes[-1], jnp.float32),
        in_specs=[vmem, vmem, pl.BlockSpec(memory_space=pl.ANY), pl.BlockSpec(memory_space=pl.ANY)],
        out_specs=vmem,
        scratch_shapes=scratch,
        compiler_params=pltpu.CompilerParams(
            collective_id=0, has_side_effects=True, vmem_limit_bytes=63 * 1024 * 1024),
    )(colors, extinction, density, bins)
    return jnp.transpose(out, (0, 2, 1))


def per_device(density, bins, colors, extinction):
    depth_cells = density.shape[0]
    slab_count = lax.axis_size("depth")
    depth_scale = 0.6 / (depth_cells * slab_count)
    return render_composite(density, bins, colors, extinction.reshape(1, -1), depth_scale,
                            slab_count.bit_length() - 1)


def solution(mesh):
    return jax.shard_map(
        per_device,
        mesh=mesh,
        in_specs=(P("depth", "tile", None), P("depth", "tile", None), P(), P()),
        out_specs=P(None, "tile", "depth"),
        check_vma=False,
    )
```
